32 devices in a mesh: shard: 8 (over z, y), tensor: 4 (over x, core).
Axes of the slice: x: 2, y: 2, z: 4, core: 2. Of those that a mesh axis runs over, the one named last changes fastest.
Arguments:
- tokens: bfloat16 [12608, 1024], P('shard'), may hold values from -6 to 6
- cotangent: bfloat16 [12608, 1024], P('shard'), may hold values from -6 to 6
- input_weight: float32 [3, 1024, 1024], P(None, 'shard', 'tensor'), may hold values from -2 to 2
- input_moments: float32 [2, 3, 1024, 1024], P(None, None, 'shard', 'tensor'), may hold values from -1 to 1, as said below
- input_bias: float32 [2, 1024], P(None, ('tensor', 'shard')), may hold values from -3 to 3
- input_bias_moments: float32 [2, 2, 1024], P(None, None, ('tensor', 'shard')), may hold values from -1 to 1, as said below
- output_weight: float32 [1024, 1024], P('tensor', 'shard'), may hold values from -0.75 to 0.75
- output_moments: float32 [2, 1024, 1024], P(None, 'tensor', 'shard'), may hold values from -1 to 1, as said below
- expand_weight: float32 [1024, 4096], P('shard', 'tensor'), may hold values from -0.1875 to 0.1875
- expand_moments: float32 [2, 1024, 4096], P(None, 'shard', 'tensor'), may hold values from -1 to 1, as said below
- expand_bias: float32 [4096], P(('tensor', 'shard')), may hold values from -3 to 3
- expand_bias_moments: float32 [2, 4096], P(None, ('tensor', 'shard')), may hold values from -1 to 1, as said below
- shrink_weight: float32 [4096, 1024], P('tensor', 'shard'), may hold values from -0.09375 to 0.09375
- shrink_moments: float32 [2, 4096, 1024], P(None, 'tensor', 'shard'), may hold values from -1 to 1, as said below
- vectors: float32 [6, 1024], P(None, 'shard'), may hold values from -1.2 to 1.4
- vector_moments: float32 [2, 6, 1024], P(None, None, 'shard'), may hold values from -1 to 1, as said below
Outputs:
- block_output: bfloat16 [12608, 1024], P('shard')
- token_gradient: float32 [12608, 1024], P('shard')
- input_weight_gradient: float32 [3, 1024, 1024], P(None, 'shard', 'tensor')
- input_bias_gradient: float32 [2, 1024], P(None, ('tensor', 'shard'))
- output_weight_gradient: float32 [1024, 1024], P('tensor', 'shard')
- expand_weight_gradient: float32 [1024, 4096], P('shard', 'tensor')
- expand_bias_gradient: float32 [4096], P(('tensor', 'shard'))
- shrink_weight_gradient: float32 [4096, 1024], P('tensor', 'shard')
- vectors_gradient: float32 [6, 1024], P(None, 'shard')
- new_input_weight: float32 [3, 1024, 1024], P(None, 'shard', 'tensor')
- new_input_bias: float32 [2, 1024], P(None, ('tensor', 'shard'))
- new_output_weight: float32 [1024, 1024], P('tensor', 'shard')
- new_expand_weight: float32 [1024, 4096], P('shard', 'tensor')
- new_expand_bias: float32 [4096], P(('tensor', 'shard'))
- new_shrink_weight: float32 [4096, 1024], P('tensor', 'shard')
- new_vectors: float32 [6, 1024], P(None, 'shard')
- new_input_moments: float32 [2, 3, 1024, 1024], P(None, None, 'shard', 'tensor')
- new_input_bias_moments: float32 [2, 2, 1024], P(None, None, ('tensor', 'shard'))
- new_output_moments: float32 [2, 1024, 1024], P(None, 'tensor', 'shard')
- new_expand_moments: float32 [2, 1024, 4096], P(None, 'shard', 'tensor')
- new_expand_bias_moments: float32 [2, 4096], P(None, ('tensor', 'shard'))
- new_shrink_moments: float32 [2, 4096, 1024], P(None, 'tensor', 'shard')
- new_vector_moments: float32 [2, 6, 1024], P(None, None, 'shard')
The draws below stay inside these ranges and needn't reach their ends.
Inputs may be any that keep to these rules, and one draw needn't show every extreme that they name: `input_moments`: second moments positive. `input_bias_moments`: second moments positive. `output_moments`: second moments positive. `expand_moments`: second moments positive. `expand_bias_moments`: second moments positive. `shrink_moments`: second moments positive. `vector_moments`: second moments positive.
All inputs are finite; a program needn't handle non-finite values.
Results may differ from the reference program's by a relative error of at most 0.015.
Values may be sent and summed in bfloat16 or wider, within the bound.
No kernel may reach another device: no remote copies, remote signals or barrier semaphores. Data moves between devices by JAX's collectives and lax.ppermute only.
A program may use at most 192 MiB of HBM per device.

```python
import math
import jax
import jax.numpy as jnp
from jax import lax

D = 1024
HEADS = 16
HEAD = 64
FF = 4096
SEQ = 197
IMG_DEV = 8
IMAGES = 64
N_SHARD = 8


def moment_pair(key, shape):
    first_key, second_key = jax.random.split(key)
    first = jax.random.uniform(first_key, shape, jnp.float32, -1.0, 1.0)
    second = jnp.exp(jax.random.uniform(second_key, shape, jnp.float32, math.log(0.05), math.log(0.5)))
    return jnp.stack([first, second])


def draw_input_weight(key, part):
    subkeys = jax.random.split(key, 1)
    base = jax.random.normal(subkeys[0], (3, D, D), jnp.float32) * D ** (-0.5)
    return jnp.clip(base, -2.0, 2.0)


def draw_vectors(key, part):
    gain_key, shift_key = jax.random.split(key)
    gains = jax.random.uniform(gain_key, (2, D), jnp.float32, 0.6, 1.4)
    shifts = jnp.clip(jax.random.normal(shift_key, (4, D), jnp.float32) * 0.3, -1.2, 1.2)
    return jnp.stack([gains[0], shifts[0], shifts[1], gains[1], shifts[2], shifts[3]])


def draw_input_moments(key, part):
    return moment_pair(key, (3, D, D))


def draw_input_bias_moments(key, part):
    return moment_pair(key, (2, D))


def draw_output_moments(key, part):
    return moment_pair(key, (D, D))


def draw_expand_moments(key, part):
    return moment_pair(key, (D, FF))


def draw_expand_bias_moments(key, part):
    return moment_pair(key, (FF,))


def draw_shrink_moments(key, part):
    return moment_pair(key, (FF, D))


def draw_vector_moments(key, part):
    return moment_pair(key, (6, D))


def level_of(own_key, dims, cuts, smallest, top_value):
    def one(position, parts):
        heights = jax.random.uniform(jax.random.fold_in(jax.random.fold_in(own_key, 6), position), (parts,), jnp.float32, smallest / len(cuts), top_value / len(cuts))
        return jnp.repeat(jnp.exp(heights), dims[position] // parts).reshape((-1,) + (1,) * (len(dims) - position - 1))

    loudness = one(*cuts[0])
    for cut in cuts[1:]:
        loudness = loudness * one(*cut)
    return loudness


def gaussian(key, dims, width, limit, cuts=(), kind=jnp.bfloat16):
    drawn = width * jax.random.normal(key, dims, jnp.float32)
    if cuts:
        drawn = drawn * level_of(key, dims, cuts, -0.22, 0.18)
    return jnp.clip(drawn, -limit, limit).astype(kind)


def setup_inputs(seed: int = 0) -> dict:
    streams_of = jax.random.split(jax.random.key(seed), 17)
    return {
        "tokens": gaussian(streams_of[0], (IMAGES * SEQ, D), 1.0, 6.0, ((0, 8),)),
        "cotangent": gaussian(streams_of[1], (IMAGES * SEQ, D), 1.0, 6.0, ((0, 8),)),
        "input_weight": draw_input_weight(jax.random.fold_in(streams_of[16], 71), 0),
        "input_moments": draw_input_moments(jax.random.fold_in(streams_of[16], 71), 0),
        "input_bias": gaussian(streams_of[4], (2, D), 0.5, 3.0, ((1, 32),), jnp.float32),
        "input_bias_moments": draw_input_bias_moments(jax.random.fold_in(streams_of[16], 71), 0),
        "output_weight": gaussian(streams_of[6], (D, D), (D // 16) ** -0.5, 0.75, ((0, 4), (1, 8)), jnp.float32),
        "output_moments": draw_output_moments(jax.random.fold_in(streams_of[16], 71), 0),
        "expand_weight": gaussian(streams_of[8], (D, FF), D ** -0.5, 0.1875, ((0, 8), (1, 4)), jnp.float32),
        "expand_moments": draw_expand_moments(jax.random.fold_in(streams_of[16], 71), 0),
        "expand_bias": gaussian(streams_of[10], (FF,), 0.5, 3.0, ((0, 32),), jnp.float32),
        "expand_bias_moments": draw_expand_bias_moments(jax.random.fold_in(streams_of[16], 71), 0),
        "shrink_weight": gaussian(streams_of[12], (FF, D), FF ** -0.5, 0.09375, ((0, 4), (1, 8)), jnp.float32),
        "shrink_moments": draw_shrink_moments(jax.random.fold_in(streams_of[16], 71), 0),
        "vectors": draw_vectors(jax.random.fold_in(streams_of[16], 71), 0),
        "vector_moments": draw_vector_moments(jax.random.fold_in(streams_of[16], 71), 0),
    }


norm_eps = 1e-06
rate = 0.003
first_decay = 0.9
second_decay = 0.95
weight_decay = 0.05
step_count = 2.0
adam_eps = 1e-08
loss_scale = 128.0

@jax.custom_vjp
def low(v):
    return lax.optimization_barrier(v.astype(jnp.bfloat16)).astype(jnp.float32)

@jax.custom_vjp
def low_back(v):
    return v

def low_keep(v):
    return (low(v), None)

def low_pass(kept, grad):
    return (grad,)

def back_keep(v):
    return (v, None)

def back_low(kept, grad):
    return (low(grad),)
low.defvjp(low_keep, low_pass)
low_back.defvjp(back_keep, back_low)

def layer_norm(values, gain, shift):
    row_mean = lax.optimization_barrier(jnp.mean(values, axis=-1, keepdims=True))
    centred = values - row_mean
    spread = lax.optimization_barrier(jnp.mean(centred * centred, axis=-1, keepdims=True))
    return centred * lax.rsqrt(spread + norm_eps) * gain + shift

def matmul(left, right):
    return jnp.dot(left, right, precision=lax.Precision.HIGHEST)

def forward(block, input_weight, input_bias, output_weight, expand_weight, expand_bias, shrink_weight, vectors):
    images = block.shape[0] // SEQ
    split_shape = (images, SEQ, HEADS, HEAD)
    normed = layer_norm(block, vectors[0], vectors[1])
    inputs = low(normed)
    project = jnp.einsum('rd,cde->cre', inputs, input_weight, precision=lax.Precision.HIGHEST)
    query = low_back(low(project[0] + input_bias[0]))
    keys = low_back(low(project[1]))
    values = low_back(low(project[2] + input_bias[1]))
    scores = jnp.einsum('gqhe,gkhe->ghqk', query.reshape(split_shape), keys.reshape(split_shape), precision=lax.Precision.HIGHEST)
    scores = low_back(scores * HEAD ** (-0.5))
    attention = low(jax.nn.softmax(scores, axis=-1))
    context = jnp.einsum('ghqk,gkhe->gqhe', attention, values.reshape(split_shape), precision=lax.Precision.HIGHEST)
    context = low_back(low(context.reshape(block.shape)))
    attended = block + low_back(matmul(context, output_weight)) + vectors[2]
    normed_mid = layer_norm(attended, vectors[3], vectors[4])
    pre_act = low_back(matmul(low(normed_mid), expand_weight) + expand_bias)
    hidden = low(jax.nn.gelu(pre_act, approximate=False))
    return attended + matmul(hidden, shrink_weight) + vectors[5]

def adamw(param, moments, grad, decay):
    scaled = grad / loss_scale
    first = first_decay * moments[0] + (1.0 - first_decay) * scaled
    second = second_decay * moments[1] + (1.0 - second_decay) * scaled * scaled
    corrected = first / (1.0 - first_decay ** step_count) / (jnp.sqrt(second / (1.0 - second_decay ** step_count)) + adam_eps)
    return (param - rate * (corrected + decay * param), jnp.stack([first, second]))

def reference(tokens, cotangent, input_weight, input_moments, input_bias, input_bias_moments, output_weight, output_moments, expand_weight, expand_moments, expand_bias, expand_bias_moments, shrink_weight, shrink_moments, vectors, vector_moments):
    rounded = (low(input_weight), low(input_bias), low(output_weight), low(expand_weight), low(expand_bias), low(shrink_weight), low(vectors))
    rows = IMG_DEV * SEQ
    blocks = tokens.astype(jnp.float32).reshape(N_SHARD, rows, D)
    back_blocks = cotangent.astype(jnp.float32).reshape(N_SHARD, rows, D)

    def one_group(totals, pair):
        block, back_block = pair
        result, pullback = jax.vjp(forward, block, *rounded)
        grads = pullback(back_block)
        totals = tuple((total + grad for total, grad in zip(totals, grads[1:])))
        return (totals, (result.astype(jnp.bfloat16), grads[0]))
    start = tuple((jnp.zeros_like(entry) for entry in rounded))
    totals, (results, token_grads) = lax.scan(one_group, start, (blocks, back_blocks))
    new_input, mom_input = adamw(input_weight, input_moments, totals[0], weight_decay)
    new_bias, mom_bias = adamw(input_bias, input_bias_moments, totals[1], 0.0)
    new_output, mom_output = adamw(output_weight, output_moments, totals[2], weight_decay)
    new_expand, mom_expand = adamw(expand_weight, expand_moments, totals[3], weight_decay)
    new_expand_bias, mom_expand_bias = adamw(expand_bias, expand_bias_moments, totals[4], 0.0)
    new_shrink, mom_shrink = adamw(shrink_weight, shrink_moments, totals[5], weight_decay)
    new_vectors, mom_vectors = adamw(vectors, vector_moments, totals[6], 0.0)
    return (results.reshape(IMAGES * SEQ, D), token_grads.reshape(IMAGES * SEQ, D), totals[0], totals[1], totals[2], totals[3], totals[4], totals[5], totals[6], new_input, new_bias, new_output, new_expand, new_expand_bias, new_shrink, new_vectors, mom_input, mom_bias, mom_output, mom_expand, mom_expand_bias, mom_shrink, mom_vectors)
```

```python
import functools

import jax
import jax.numpy as jnp
from jax import lax
from jax.experimental import pallas as pl
from jax.experimental.pallas import tpu as pltpu
from jax.sharding import PartitionSpec as P

HEAD = 64
SEQ = 197
PAD = 208
LANES = 128

norm_eps = 1e-06
rate = 0.003
first_decay = 0.9
second_decay = 0.95
weight_decay = 0.05
step_count = 2.0
adam_eps = 1e-08
loss_scale = 128.0

bf16 = jnp.bfloat16
f32 = jnp.float32
NT = (((1,), (1,)), ((), ()))
TN = (((0,), (0,)), ((), ()))
PARAMS = pltpu.CompilerParams(vmem_limit_bytes=60 * 1024 * 1024)


def dot(left, right):
    return jnp.dot(left, right, preferred_element_type=f32)


def dot_nt(left, right):
    return lax.dot_general(left, right, NT, preferred_element_type=f32)


def dot_tn(left, right):
    return lax.dot_general(left, right, TN, preferred_element_type=f32)


def whole(shape):
    return pl.BlockSpec(shape, lambda i, idx: (0,) * len(shape))


def picked(shape):
    return pl.BlockSpec((1,) + shape, lambda i, idx: (idx[i],) + (0,) * len(shape))


def store_one(refs, i, value):
    for j, ref in enumerate(refs):

        @pl.when(i == j)
        def _():
            ref[...] = value


def load_one(refs, i, scratch):
    for j, ref in enumerate(refs):

        @pl.when(i == j)
        def _():
            scratch[...] = ref[...]

    return scratch[...]


def norm_stats(values):
    centred = values - jnp.mean(values, axis=-1, keepdims=True)
    spread = jnp.mean(centred * centred, axis=-1, keepdims=True)
    inverse = lax.rsqrt(spread + norm_eps)
    return centred * inverse, inverse


def norm_back(unit, inverse, grad, gain):
    scaled = grad * gain
    mean_one = jnp.mean(scaled, axis=-1, keepdims=True)
    mean_two = jnp.mean(scaled * unit, axis=-1, keepdims=True)
    return inverse * (scaled - mean_one - unit * mean_two)


def attn_fwd_kernel(nq, width, shared, idx, tok, w, vec, bias, *rest):
    rest = rest[shared:]
    inputs_out, qkv_out, ctx_out = rest[:3]
    parts = rest[3:]
    i = pl.program_id(0)
    unit, _ = norm_stats(tok[0].astype(f32))
    inputs = (unit * vec[0:1, :] + vec[1:2, :]).astype(bf16)
    inputs_out[0] = inputs
    project = dot(inputs, w[:, : 3 * width])
    query = (project[:, :width] + bias[0:1, :]).astype(bf16)
    keys = project[:, width : 2 * width].astype(bf16)
    values = (project[:, 2 * width :] + bias[1:2, :]).astype(bf16)
    qkv_out[0, :, :width] = query
    qkv_out[0, :, width : 2 * width] = keys
    qkv_out[0, :, 2 * width :] = values
    scale = bf16(HEAD ** (-0.5))
    lane = lax.broadcasted_iota(jnp.int32, (1, LANES), 1)
    live = lax.broadcasted_iota(jnp.int32, (1, PAD), 1) < SEQ
    for image in range(tok.shape[1] // PAD):
        rows = slice(image * PAD, (image + 1) * PAD)
        for pair in range(width // LANES):
            cols = slice(pair * LANES, (pair + 1) * LANES)
            q2, k2, v2 = query[rows, cols] * scale, keys[rows, cols], values[rows, cols]
            outs = []
            for half in range(LANES // HEAD):
                mine = (lane // HEAD) == half
                scores = dot_nt(jnp.where(mine, q2, bf16(0)), k2)
                scores = jnp.where(live, scores, -1e30)
                raised = jnp.exp(scores - jnp.max(scores, axis=-1, keepdims=True))
                total = jnp.sum(raised, axis=-1, keepdims=True)
                outs.append(dot((raised * (1.0 / total)).astype(bf16), v2))
            ctx_out[0, rows, cols] = jnp.where(lane < HEAD, outs[0], outs[1]).astype(bf16)
    store_one(parts, i, dot_nt(ctx_out[0], w[:, 3 * width : 4 * width]).astype(bf16))


def ffn_kernel(nq, shared, idx, *refs):
    pieces, (cot, w, bias) = refs[:nq], refs[nq : nq + 3]
    refs = refs[nq + 3 + shared :]
    x_out, hid_out, pre_out, bias_out = refs[:4]
    shrink_parts, mid_parts, scratch = refs[4 : 4 + nq], refs[4 + nq : 4 + 2 * nq], refs[-1]
    i = pl.program_id(0)
    width = bias.shape[1]
    x = load_one(pieces, i, scratch)
    x_out[0] = x
    back = cot[0]

    @pl.when(i == 0)
    def _():
        bias_out[...] = jnp.zeros_like(bias_out)

    step = 256
    for start in range(0, width, step):
        cols = slice(start, start + step)
        second = slice(width + start, width + start + step)
        pre = dot(x, w[:, cols]) + bias[0:1, cols]
        grad = dot(back, w[:, second])
        share = 0.5 + 0.5 * lax.erf(pre * (0.5**0.5))
        slope = share + pre * (jnp.exp(-0.5 * pre * pre) * 0.3989422804014327)
        hid_out[0, :, cols] = (pre * share).astype(bf16)
        pre_grad = (slope * grad).astype(bf16)
        pre_out[0, :, cols] = pre_grad
        bias_out[0:1, cols] += jnp.sum(pre_grad.astype(f32), axis=0, keepdims=True)
    store_one(shrink_parts, i, dot_nt(hid_out[0], w[:, width:]).astype(bf16))
    store_one(mid_parts, i, dot_nt(pre_out[0], w[:, :width]).astype(bf16))


def attn_bwd_kernel(nq, width, shared, idx, *refs):
    pieces, (tok, qkv, w) = refs[:nq], refs[nq : nq + 3]
    refs = refs[nq + 3 + shared :]
    mid_out, grad_out, sums_out, vec_out = refs[:4]
    parts, scratch = refs[4 : 4 + nq], refs[-1]
    i = pl.program_id(0)
    mid = load_one(pieces, i, scratch)
    mid_out[0] = mid
    ctx_grad = dot(mid, w[:, 3 * width : 4 * width]).astype(bf16)
    scale = bf16(HEAD ** (-0.5))
    lane = lax.broadcasted_iota(jnp.int32, (1, LANES), 1)
    live = lax.broadcasted_iota(jnp.int32, (PAD, 1), 0) < SEQ
    for image in range(tok.shape[1] // PAD):
        rows = slice(image * PAD, (image + 1) * PAD)
        for pair in range(width // LANES):
            at = [slice(c * width + pair * LANES, c * width + (pair + 1) * LANES) for c in range(3)]
            q2, k2, v2 = qkv[0, rows, at[0]] * scale, qkv[0, rows, at[1]], qkv[0, rows, at[2]]
            c2 = ctx_grad[rows, pair * LANES : (pair + 1) * LANES]
            outs = []
            for half in range(LANES // HEAD):
                mine = (lane // HEAD) == half
                scores = dot_nt(k2, jnp.where(mine, q2, bf16(0)))
                scores = jnp.where(live, scores, -1e30)
                raised = jnp.exp(scores - jnp.max(scores, axis=0, keepdims=True))
                prob = raised * (1.0 / jnp.sum(raised, axis=0, keepdims=True))
                prob_grad = dot_nt(v2, jnp.where(mine, c2, bf16(0)))
                row_dot = jnp.sum(prob_grad * prob, axis=0, keepdims=True)
                score_grad = (prob * (prob_grad - row_dot)).astype(bf16)
                outs.append(
                    (
                        dot_tn(score_grad, k2) * HEAD ** (-0.5),
                        dot(score_grad, q2),
                        dot(prob.astype(bf16), c2),
                    )
                )
            for c in range(3):
                grad_out[0, rows, at[c]] = jnp.where(lane < HEAD, outs[0][c], outs[1][c]).astype(bf16)
    grads = grad_out[0]
    part = dot_nt(grads, w[:, : 3 * width])
    store_one(parts, i, part.astype(bf16))
    unit, _ = norm_stats(tok[0].astype(f32))

    @pl.when(i == 0)
    def _():
        sums_out[...] = jnp.zeros_like(sums_out)
        vec_out[...] = jnp.zeros_like(vec_out)

    sums_out[0:1, :] += jnp.sum(grads.astype(f32), axis=0, keepdims=True)
    vec_out[0:1, :] += jnp.sum(part * unit, axis=0, keepdims=True)
    vec_out[1:2, :] += jnp.sum(part, axis=0, keepdims=True)


def mid_kernel(idx, tok, mine, theirs, vec, attended_out, normed_out):
    attended = tok[0].astype(f32) + (mine[...].astype(f32) + theirs[...].astype(f32)) + vec[2:3, :]
    attended_out[...] = attended
    unit, _ = norm_stats(attended)
    normed_out[...] = (unit * vec[3:4, :] + vec[4:5, :]).astype(bf16)


def mid_back_kernel(idx, attended, cot, mine, theirs, vec, mid_out, low_out, sums_out):
    grad = mine[...].astype(f32) + theirs[...].astype(f32)
    unit, inverse = norm_stats(attended[...])
    back = cot[0].astype(f32)
    mid = back + norm_back(unit, inverse, grad, vec[3:4, :])
    mid_out[...] = mid
    low_out[...] = mid.astype(bf16)
    sums_out[...] = jnp.zeros_like(sums_out)
    sums_out[0:1, :] = jnp.sum(mid, axis=0, keepdims=True)
    sums_out[1:2, :] = jnp.sum(grad * unit, axis=0, keepdims=True)
    sums_out[2:3, :] = jnp.sum(grad, axis=0, keepdims=True)
    sums_out[3:4, :] = jnp.sum(back, axis=0, keepdims=True)


def token_back_kernel(idx, tok, mid, mine, theirs, vec, out):
    grad = mine[...].astype(f32) + theirs[...].astype(f32)
    unit, inverse = norm_stats(tok[0].astype(f32))
    out[...] = (mid[...] + norm_back(unit, inverse, grad, vec[0:1, :])).astype(bf16)


def spread_kernel(nq, idx, *refs):
    pieces, out = refs[:nq], refs[nq]
    i = pl.program_id(0)
    for j, piece in enumerate(pieces):

        @pl.when(i == j)
        def _():
            for image in range(out.shape[0]):
                out[image] = piece[image * PAD : image * PAD + SEQ, :].astype(out.dtype)


def weight_grad_kernel(idx, left_one, right_one, left_two, right_two, tail, out):
    first, second = right_one.shape[1], right_two.shape[1]
    out[:, :first] = dot_tn(left_one[...], right_one[...]).astype(bf16)
    out[:, first : first + second] = dot_tn(left_two[...], right_two[...]).astype(bf16)
    if out.shape[1] > first + second:
        out[:, first + second :] = tail[...]


def call(kernel, grid, idx, in_specs, out_specs, out_shapes, args, aliases=None, scratch=(), name=None):
    return pl.pallas_call(
        kernel,
        grid_spec=pltpu.PrefetchScalarGridSpec(
            num_scalar_prefetch=1,
            grid=grid,
            in_specs=in_specs,
            out_specs=out_specs,
            scratch_shapes=list(scratch),
        ),
        out_shape=out_shapes,
        input_output_aliases=aliases or {},
        compiler_params=PARAMS,
        name=name,
    )(idx, *args)


def sds(shape, dtype):
    return jax.ShapeDtypeStruct(shape, dtype)


def shared_args(buffers, n_args):
    specs = [pl.BlockSpec(memory_space=pl.ANY)] * len(buffers)
    aliases = {1 + n_args + j: j for j in range(len(buffers))}
    return specs, list(buffers), aliases


def attn_fwd(idx, tok, w, vec, bias, buffers):
    nq, (quarters, rows, d), width = idx.shape[0], tok.shape, bias.shape[1]
    specs, extra, aliases = shared_args(buffers, 4)
    out = call(
        functools.partial(attn_fwd_kernel, nq, width, len(buffers)),
        (nq,),
        idx,
        [picked((rows, d)), whole(w.shape), whole(vec.shape), whole(bias.shape)] + specs,
        [picked((rows, d)), picked((rows, 3 * width)), picked((rows, width))] + [whole((rows, d))] * nq,
        [sds((quarters, rows, n), bf16) for n in (d, 3 * width, width)] + [sds((rows, d), bf16)] * nq,
        [tok, w, vec, bias] + extra,
        aliases,
        name="attention_forward",
    )
    return out[:3], out[3:]


def ffn(idx, pieces, cot, w, bias, buffers):
    nq, (quarters, rows, d), width = idx.shape[0], cot.shape, bias.shape[1]
    specs, extra, aliases = shared_args(buffers, nq + 3)
    out = call(
        functools.partial(ffn_kernel, nq, len(buffers)),
        (nq,),
        idx,
        [whole((rows, d))] * nq + [picked((rows, d)), whole(w.shape), whole(bias.shape)] + specs,
        [picked((rows, d)), picked((rows, width)), picked((rows, width)), whole((8, width))]
        + [whole((rows, d))] * (2 * nq),
        [sds((quarters, rows, n), bf16) for n in (d, width, width)]
        + [sds((8, width), f32)]
        + [sds((rows, d), bf16)] * (2 * nq),
        list(pieces) + [cot, w, bias] + extra,
        aliases,
        [pltpu.VMEM((rows, d), bf16)],
        name="feed_forward",
    )
    return out[:3], out[3][0], out[4 : 4 + nq], out[4 + nq :]


def attn_bwd(idx, pieces, tok, qkv, w, buffers):
    nq, (quarters, rows, d), width = idx.shape[0], tok.shape, qkv.shape[2] // 3
    specs, extra, aliases = shared_args(buffers, nq + 3)
    out = call(
        functools.partial(attn_bwd_kernel, nq, width, len(buffers)),
        (nq,),
        idx,
        [whole((rows, d))] * nq + [picked((rows, d)), picked((rows, 3 * width)), whole(w.shape)] + specs,
        [picked((rows, d)), picked((rows, 3 * width)), whole((8, 3 * width)), whole((8, d))]
        + [whole((rows, d))] * nq,
        [sds((quarters, rows, d), bf16), sds((quarters, rows, 3 * width), bf16)]
        + [sds((8, 3 * width), f32), sds((8, d), f32)]
        + [sds((rows, d), bf16)] * nq,
        list(pieces) + [tok, qkv, w] + extra,
        aliases,
        [pltpu.VMEM((rows, d), bf16)],
        name="attention_backward",
    )
    return out[:2], out[2][0], out[3][:2], out[4:]


def rowwise(kernel, idx, args, specs, outs, name):
    return call(kernel, (1,), idx, specs, [whole(o.shape) for o in outs], outs, args, name=name)


def weight_grads(idx, left_one, right_one, left_two, right_two, tail, name):
    d = left_one.shape[2]
    flat = [v.reshape(-1, v.shape[2]) for v in (left_one, right_one, left_two, right_two)]
    first, second = flat[1].shape[1], flat[3].shape[1]
    extra = 0 if tail is None else tail.shape[1]
    tail = jnp.zeros((d, LANES), bf16) if tail is None else tail
    step = 256
    n = flat[0].shape[0]
    column = pl.BlockSpec((n, step), lambda i, idx: (0, i))
    return call(
        weight_grad_kernel,
        (d // step,),
        idx,
        [column, whole((n, first)), column, whole((n, second)), pl.BlockSpec((step, LANES), lambda i, idx: (i, 0))],
        pl.BlockSpec((step, first + second + extra), lambda i, idx: (i, 0)),
        sds((d, first + second + extra), bf16),
        flat + [tail],
        name=name,
    )


def spread(idx, pieces, dtype, name):
    rows, d = pieces[0].shape
    images = rows // PAD
    nq = len(pieces)
    out = call(
        functools.partial(spread_kernel, nq),
        (nq,),
        idx,
        [whole((rows, d))] * nq,
        pl.BlockSpec((images, SEQ, d), lambda i, idx: (idx[i], 0, 0)),
        sds((nq * images, SEQ, d), dtype),
        list(pieces),
        name=name,
    )
    return out.reshape(-1, d)


def swap(value, flip, size):
    return lax.ppermute(value, "tensor", [(k, k ^ flip) for k in range(size)])


def add_low(left, right):
    return (left.astype(f32) + right.astype(f32)).astype(bf16)


def adamw(param, moments, grad, decay):
    scaled = grad / loss_scale
    first = first_decay * moments[0] + (1.0 - first_decay) * scaled
    second = second_decay * moments[1] + (1.0 - second_decay) * scaled * scaled
    corrected = (
        first
        / (1.0 - first_decay**step_count)
        / (jnp.sqrt(second / (1.0 - second_decay**step_count)) + adam_eps)
    )
    return (param - rate * (corrected + decay * param), jnp.stack([first, second]))


def on_device(
    n_shard,
    n_tensor,
    tokens,
    cotangent,
    input_weight,
    input_moments,
    input_bias,
    input_bias_moments,
    output_weight,
    output_moments,
    expand_weight,
    expand_moments,
    expand_bias,
    expand_bias_moments,
    shrink_weight,
    shrink_moments,
    vectors,
    vector_moments,
):
    rows, d = tokens.shape
    images = rows // SEQ
    per = images // n_tensor
    part = d // n_shard
    width = input_weight.shape[2]
    hidden = expand_weight.shape[1]
    me = lax.axis_index("tensor").astype(jnp.int32)
    index = jnp.arange(n_tensor, dtype=jnp.int32) ^ me
    near, far, own = index[:2], index[2:], index[:1]

    small = jnp.concatenate([vectors, expand_bias.reshape(1, -1)], axis=0)
    small = jnp.pad(small, ((0, 0), (0, LANES - part)))
    bias_rows = jnp.pad(input_bias, ((0, 0), (0, LANES - input_bias.shape[1])))
    small = jnp.concatenate([small, bias_rows], axis=0)
    n_small = small.shape[0]
    small = jnp.pad(small, ((0, part - n_small), (0, 0)))
    pack_one = jnp.concatenate(
        [input_weight[c] for c in range(3)] + [output_weight.T, small], axis=1
    ).astype(bf16)
    pack_two = jnp.concatenate([expand_weight, shrink_weight.T], axis=1).astype(bf16)
    w_one = lax.all_gather(pack_one, "shard", axis=0, tiled=True)
    w_two = lax.all_gather(pack_two, "shard", axis=0, tiled=True)
    small = w_one[:, 4 * width :].reshape(n_shard, part, LANES)[:, :n_small].astype(f32)
    vec = jnp.pad(small[:, :6, :part].transpose(1, 0, 2).reshape(6, d), ((0, 2), (0, 0)))
    full_expand_bias = small[:, 6, :part].reshape(1, hidden)
    full_bias = small[:, 7:9, : width // n_shard].transpose(1, 0, 2).reshape(2, width)

    def padded(values):
        values = values.reshape(images, SEQ, d)
        values = jnp.pad(values, ((0, 0), (0, PAD - SEQ), (0, 0)))
        return values.reshape(n_tensor, per * PAD, d)

    tok, cot = padded(tokens), padded(cotangent)
    q_rows = per * PAD
    block = (q_rows, d)

    buffers, (p2, p3) = attn_fwd(far, tok, w_one, vec, full_bias, ())
    sum2 = add_low(p2, swap(p3, 1, n_tensor))
    cross = swap(sum2, 2, n_tensor)
    (inputs_all, qkv_all, ctx_all), (p0, p1) = attn_fwd(near, tok, w_one, vec, full_bias, buffers)
    sum0 = add_low(p0, swap(p1, 1, n_tensor))
    attended, normed = rowwise(
        mid_kernel,
        own,
        [tok, sum0, cross, vec],
        [picked(block), whole(block), whole(block), whole(vec.shape)],
        [sds(block, f32), sds(block, bf16)],
        "middle_forward",
    )

    def gather_rows(value):
        over = swap(value, 2, n_tensor)
        return (value, swap(value, 1, n_tensor)), (over, swap(over, 1, n_tensor))

    near_x, far_x = gather_rows(normed)
    buffers, bias_near, shrink_near, mid_near = ffn(near, near_x, cot, w_two, full_expand_bias, ())
    ffn_all, bias_far, shrink_far, mid_far = ffn(far, far_x, cot, w_two, full_expand_bias, buffers)
    x_all, hid_all, pre_all = ffn_all

    def scatter_rows(near_parts, far_parts):
        over = add_low(far_parts[0], swap(far_parts[1], 1, n_tensor))
        over = swap(over, 2, n_tensor)
        return add_low(near_parts[0], swap(near_parts[1], 1, n_tensor)), over

    mid_mine, mid_theirs = scatter_rows(mid_near, mid_far)
    mid, mid_low, vec_mid = rowwise(
        mid_back_kernel,
        own,
        [attended, cot, mid_mine, mid_theirs, vec],
        [whole(block), picked(block), whole(block), whole(block), whole(vec.shape)],
        [sds(block, f32), sds(block, bf16), sds((8, d), f32)],
        "middle_backward",
    )
    grads_two = weight_grads(own, x_all, pre_all, cot, hid_all, None, "feed_forward_weights")
    share_two = lax.psum_scatter(grads_two, "shard", scatter_dimension=0, tiled=True)

    near_m, far_m = gather_rows(mid_low)
    buffers, sums_near, vec_near, part_near = attn_bwd(near, near_m, tok, qkv_all, w_one, ())
    (mid_all, grad_all), sums_far, vec_far, part_far = attn_bwd(far, far_m, tok, qkv_all, w_one, buffers)

    vec_grads = jnp.concatenate([vec_near + vec_far, vec_mid[:4], (bias_near + bias_far).reshape(1, d)])
    vec_grads = vec_grads.reshape(7, n_shard, part).transpose(1, 0, 2)
    vec_grads = jnp.pad(vec_grads, ((0, 0), (0, 0), (0, LANES - part)))
    sums = sums_near + sums_far
    bias_grads = jnp.stack([sums[:width], sums[2 * width :]]).reshape(2, n_shard, -1).transpose(1, 0, 2)
    bias_grads = jnp.pad(bias_grads, ((0, 0), (0, 0), (0, LANES - bias_grads.shape[2])))
    tail = jnp.concatenate([vec_grads, bias_grads], axis=1)
    tail = jnp.pad(tail, ((0, 0), (0, part - n_small), (0, 0))).reshape(d, LANES).astype(bf16)
    grads_one = weight_grads(own, inputs_all, grad_all, mid_all, ctx_all, tail, "attention_weights")
    share_one = lax.psum_scatter(grads_one, "shard", scatter_dimension=0, tiled=True)

    mine, theirs = scatter_rows(part_near, part_far)
    (token_low,) = rowwise(
        token_back_kernel,
        own,
        [tok, mid, mine, theirs, vec],
        [picked(block), whole(block), whole(block), whole(block), whole(vec.shape)],
        [sds(block, bf16)],
        "token_backward",
    )
    near_t, far_t = gather_rows(token_low)
    token_gradient = spread(index, near_t + far_t, f32, "token_gradient")

    shrink_mine, shrink_theirs = scatter_rows(shrink_near, shrink_far)
    result = attended + (shrink_mine.astype(f32) + shrink_theirs.astype(f32)) + vec[5]
    near_o, far_o = gather_rows(result.astype(bf16))
    block_output = spread(index, near_o + far_o, bf16, "block_output")

    share_one, share_two = share_one.astype(f32), share_two.astype(f32)
    share_input = jnp.stack([share_one[:, c * width : (c + 1) * width] for c in range(3)])
    share_output = share_one[:, 3 * width : 4 * width].T
    share_expand = share_two[:, :hidden]
    share_shrink = share_two[:, hidden:].T
    small = share_one[:n_small, 4 * width :]
    share_vectors = small[:6, :part]
    share_vectors = share_vectors + swap(share_vectors, 1, n_tensor)
    share_vectors = share_vectors + swap(share_vectors, 2, n_tensor)
    share_expand_bias = small[6, :part]
    share_bias = small[7:9, : width // n_shard]

    new_input, mom_input = adamw(input_weight, input_moments, share_input, weight_decay)
    new_bias, mom_bias = adamw(input_bias, input_bias_moments, share_bias, 0.0)
    new_output, mom_output = adamw(output_weight, output_moments, share_output, weight_decay)
    new_expand, mom_expand = adamw(expand_weight, expand_moments, share_expand, weight_decay)
    new_expand_bias, mom_expand_bias = adamw(
        expand_bias, expand_bias_moments, share_expand_bias, 0.0
    )
    new_shrink, mom_shrink = adamw(shrink_weight, shrink_moments, share_shrink, weight_decay)
    new_vectors, mom_vectors = adamw(vectors, vector_moments, share_vectors, 0.0)
    return (
        block_output,
        token_gradient,
        share_input,
        share_bias,
        share_output,
        share_expand,
        share_expand_bias,
        share_shrink,
        share_vectors,
        new_input,
        new_bias,
        new_output,
        new_expand,
        new_expand_bias,
        new_shrink,
        new_vectors,
        mom_input,
        mom_bias,
        mom_output,
        mom_expand,
        mom_expand_bias,
        mom_shrink,
        mom_vectors,
    )


def solution(mesh):
    return jax.shard_map(
        functools.partial(on_device, mesh.shape["shard"], mesh.shape["tensor"]),
        mesh=mesh,
        in_specs=(
            P("shard", None),
            P("shard", None),
            P(None, "shard", "tensor"),
            P(None, None, "shard", "tensor"),
            P(None, ("tensor", "shard")),
            P(None, None, ("tensor", "shard")),
            P("tensor", "shard"),
            P(None, "tensor", "shard"),
            P("shard", "tensor"),
            P(None, "shard", "tensor"),
            P(("tensor", "shard")),
            P(None, ("tensor", "shard")),
            P("tensor", "shard"),
            P(None, "tensor", "shard"),
            P(None, "shard"),
            P(None, None, "shard"),
        ),
        out_specs=(
            P("shard", None),
            P("shard", None),
            P(None, "shard", "tensor"),
            P(None, ("tensor", "shard")),
            P("tensor", "shard"),
            P("shard", "tensor"),
            P(("tensor", "shard")),
            P("tensor", "shard"),
            P(None, "shard"),
            P(None, "shard", "tensor"),
            P(None, ("tensor", "shard")),
            P("tensor", "shard"),
            P("shard", "tensor"),
            P(("tensor", "shard")),
            P("tensor", "shard"),
            P(None, "shard"),
            P(None, None, "shard", "tensor"),
            P(None, None, ("tensor", "shard")),
            P(None, "tensor", "shard"),
            P(None, "shard", "tensor"),
            P(None, ("tensor", "shard")),
            P(None, "tensor", "shard"),
            P(None, None, "shard"),
        ),
        check_vma=False,
    )
```

```python
import functools

import jax
import jax.numpy as jnp
from jax import lax
from jax.experimental import pallas as pl
from jax.experimental.pallas import tpu as pltpu
from jax.sharding import PartitionSpec as P


HEAD = 64
SEQ = 197
PAD = 208
LANES = 128
SHARD, TENSOR = "shard", "tensor"

norm_eps = 1e-06
rate = 0.003
first_decay = 0.9
second_decay = 0.95
weight_decay = 0.05
step_count = 2.0
adam_eps = 1e-08
loss_scale = 128.0


bf16 = jnp.bfloat16
f32 = jnp.float32
NT = (((1,), (1,)), ((), ()))
TN = (((0,), (0,)), ((), ()))
PARAMS = pltpu.CompilerParams(vmem_limit_bytes=40 * 1024 * 1024)


def dot(left, right):
    return jnp.dot(left, right, preferred_element_type=f32)


def dot_nt(left, right):
    return lax.dot_general(left, right, NT, preferred_element_type=f32)


def dot_tn(left, right):
    return lax.dot_general(left, right, TN, preferred_element_type=f32)


def whole(shape):
    return pl.BlockSpec(shape, lambda i, idx: (0,) * len(shape))


def picked(shape):
    return pl.BlockSpec((1,) + shape, lambda i, idx: (idx[i],) + (0,) * len(shape))


def store_one(refs, i, value):
    for j, ref in enumerate(refs):

        @pl.when(i == j)
        def _():
            ref[...] = value


def load_one(refs, i, scratch):
    for j, ref in enumerate(refs):

        @pl.when(i == j)
        def _():
            scratch[...] = ref[...]

    return scratch[...]


def norm_stats(values):
    centred = values - jnp.mean(values, axis=-1, keepdims=True)
    spread = jnp.mean(centred * centred, axis=-1, keepdims=True)
    inverse = lax.rsqrt(spread + norm_eps)
    return centred * inverse, inverse


def norm_back(unit, inverse, grad, gain):
    scaled = grad * gain
    mean_one = jnp.mean(scaled, axis=-1, keepdims=True)
    mean_two = jnp.mean(scaled * unit, axis=-1, keepdims=True)
    return inverse * (scaled - mean_one - unit * mean_two)


def attn_fwd_kernel(width, shared, idx, tok, w, vec, bias, *rest):
    rest = rest[shared:]
    inputs_out, qkv_out, ctx_out = rest[:3]
    parts = rest[3:]
    i = pl.program_id(0)
    unit, _ = norm_stats(tok[0].astype(f32))
    inputs = (unit * vec[0:1, :] + vec[1:2, :]).astype(bf16)
    inputs_out[0] = inputs
    project = dot(inputs, w[:, : 3 * width])
    query = (project[:, :width] + bias[0:1, :]).astype(bf16)
    keys = project[:, width : 2 * width].astype(bf16)
    values = (project[:, 2 * width :] + bias[1:2, :]).astype(bf16)
    qkv_out[0, :, :width] = query
    qkv_out[0, :, width : 2 * width] = keys
    qkv_out[0, :, 2 * width :] = values
    scale = bf16(HEAD ** (-0.5))
    lane = lax.broadcasted_iota(jnp.int32, (1, LANES), 1)
    live = lax.broadcasted_iota(jnp.int32, (1, PAD), 1) < SEQ

    def one_image(image, _):
        rows = pl.ds(pl.multiple_of(image * PAD, PAD), PAD)
        for pair in range(width // LANES):
            at = [slice(c * width + pair * LANES, c * width + (pair + 1) * LANES) for c in range(3)]
            q2, k2, v2 = qkv_out[0, rows, at[0]] * scale, qkv_out[0, rows, at[1]], qkv_out[0, rows, at[2]]
            outs = []
            for half in range(LANES // HEAD):
                mine = (lane // HEAD) == half
                scores = dot_nt(jnp.where(mine, q2, bf16(0)), k2)
                scores = jnp.where(live, scores, -1e30)
                raised = jnp.exp(scores - jnp.max(scores, axis=-1, keepdims=True))
                total = jnp.sum(raised, axis=-1, keepdims=True)
                outs.append(dot((raised * (1.0 / total)).astype(bf16), v2))
            ctx_out[0, rows, at[0]] = jnp.where(lane < HEAD, outs[0], outs[1]).astype(bf16)
        return 0

    lax.fori_loop(0, tok.shape[1] // PAD, one_image, 0)
    store_one(parts, i, dot_nt(ctx_out[0], w[:, 3 * width : 4 * width]).astype(bf16))


def ffn_kernel(nq, shared, idx, *refs):
    pieces, (cot, w, bias) = refs[:nq], refs[nq : nq + 3]
    refs = refs[nq + 3 + shared :]
    x_out, hid_out, pre_out, bias_out = refs[:4]
    shrink_parts, mid_parts, scratch = refs[4 : 4 + nq], refs[4 + nq : 4 + 2 * nq], refs[-1]
    i = pl.program_id(0)
    width = bias.shape[1]
    x = load_one(pieces, i, scratch)
    x_out[0] = x
    back = cot[0]

    @pl.when(i == 0)
    def _():
        bias_out[...] = jnp.zeros_like(bias_out)

    step = 512

    def some_columns(k, _):
        start = pl.multiple_of(k * step, step)
        cols, second = pl.ds(start, step), pl.ds(width + start, step)
        pre = dot(x, w[:, cols]) + bias[0:1, cols]
        grad = dot(back, w[:, second])
        share = 0.5 + 0.5 * lax.erf(pre * (0.5**0.5))
        slope = share + pre * (jnp.exp(-0.5 * pre * pre) * 0.3989422804014327)
        hid_out[0, :, cols] = (pre * share).astype(bf16)
        pre_grad = (slope * grad).astype(bf16)
        pre_out[0, :, cols] = pre_grad
        bias_out[0:1, cols] += jnp.sum(pre_grad.astype(f32), axis=0, keepdims=True)
        return 0

    lax.fori_loop(0, width // step, some_columns, 0)
    store_one(shrink_parts, i, dot_nt(hid_out[0], w[:, width:]).astype(bf16))
    store_one(mid_parts, i, dot_nt(pre_out[0], w[:, :width]).astype(bf16))


def attn_bwd_kernel(nq, width, shared, idx, *refs):
    pieces, (tok, qkv, w) = refs[:nq], refs[nq : nq + 3]
    refs = refs[nq + 3 + shared :]
    mid_out, grad_out, sums_out, vec_out = refs[:4]
    parts, scratch, ctx_grads = refs[4 : 4 + nq], refs[-2], refs[-1]
    i = pl.program_id(0)
    mid = load_one(pieces, i, scratch)
    mid_out[0] = mid
    ctx_grad = dot(mid, w[:, 3 * width : 4 * width]).astype(bf16)
    scale = bf16(HEAD ** (-0.5))
    lane = lax.broadcasted_iota(jnp.int32, (1, LANES), 1)
    live = lax.broadcasted_iota(jnp.int32, (PAD, 1), 0) < SEQ

    ctx_grads[...] = ctx_grad

    def one_image(image, _):
        rows = pl.ds(pl.multiple_of(image * PAD, PAD), PAD)
        for pair in range(width // LANES):
            at = [slice(c * width + pair * LANES, c * width + (pair + 1) * LANES) for c in range(3)]
            q2, k2, v2 = qkv[0, rows, at[0]] * scale, qkv[0, rows, at[1]], qkv[0, rows, at[2]]
            c2 = ctx_grads[rows, pair * LANES : (pair + 1) * LANES]
            outs = []
            for half in range(LANES // HEAD):
                mine = (lane // HEAD) == half
                scores = dot_nt(k2, jnp.where(mine, q2, bf16(0)))
                scores = jnp.where(live, scores, -1e30)
                raised = jnp.exp(scores - jnp.max(scores, axis=0, keepdims=True))
                prob = raised * (1.0 / jnp.sum(raised, axis=0, keepdims=True))
                prob_grad = dot_nt(v2, jnp.where(mine, c2, bf16(0)))
                row_dot = jnp.sum(prob_grad * prob, axis=0, keepdims=True)
                score_grad = (prob * (prob_grad - row_dot)).astype(bf16)
                outs.append(
                    (
                        dot_tn(score_grad, k2) * HEAD ** (-0.5),
                        dot(score_grad, q2),
                        dot(prob.astype(bf16), c2),
                    )
                )
            for c in range(3):
                grad_out[0, rows, at[c]] = jnp.where(lane < HEAD, outs[0][c], outs[1][c]).astype(bf16)
        return 0

    lax.fori_loop(0, tok.shape[1] // PAD, one_image, 0)
    grads = grad_out[0]
    part = dot_nt(grads, w[:, : 3 * width])
    store_one(parts, i, part.astype(bf16))
    unit, _ = norm_stats(tok[0].astype(f32))

    @pl.when(i == 0)
    def _():
        sums_out[...] = jnp.zeros_like(sums_out)
        vec_out[...] = jnp.zeros_like(vec_out)

    sums_out[0:1, :] += jnp.sum(grads.astype(f32), axis=0, keepdims=True)
    vec_out[0:1, :] += jnp.sum(part * unit, axis=0, keepdims=True)
    vec_out[1:2, :] += jnp.sum(part, axis=0, keepdims=True)


def mid_kernel(idx, tok, mine, theirs, vec, attended_out, normed_out):
    attended = tok[0].astype(f32) + (mine[...].astype(f32) + theirs[...].astype(f32)) + vec[2:3, :]
    attended_out[...] = attended
    unit, _ = norm_stats(attended)
    normed_out[...] = (unit * vec[3:4, :] + vec[4:5, :]).astype(bf16)


def mid_back_kernel(idx, attended, cot, mine, theirs, vec, mid_out, low_out, sums_out):
    grad = mine[...].astype(f32) + theirs[...].astype(f32)
    unit, inverse = norm_stats(attended[...])
    back = cot[0].astype(f32)
    mid = back + norm_back(unit, inverse, grad, vec[3:4, :])
    mid_out[...] = mid
    low_out[...] = mid.astype(bf16)

    @pl.when(pl.program_id(0) == 0)
    def _():
        sums_out[...] = jnp.zeros_like(sums_out)

    sums_out[0:1, :] += jnp.sum(mid, axis=0, keepdims=True)
    sums_out[1:2, :] += jnp.sum(grad * unit, axis=0, keepdims=True)
    sums_out[2:3, :] += jnp.sum(grad, axis=0, keepdims=True)
    sums_out[3:4, :] += jnp.sum(back, axis=0, keepdims=True)


def token_back_kernel(idx, tok, mid, mine, theirs, vec, out):
    grad = mine[...].astype(f32) + theirs[...].astype(f32)
    unit, inverse = norm_stats(tok[0].astype(f32))
    out[...] = (mid[...] + norm_back(unit, inverse, grad, vec[0:1, :])).astype(bf16)


def spread_kernel(nq, idx, *refs):
    pieces, out, flat = refs[:nq], refs[nq], refs[nq + 1]

    def some_columns(k, _):
        cols = pl.ds(pl.multiple_of(k * LANES, LANES), LANES)
        for j, piece in enumerate(pieces):
            images = piece.shape[0] // PAD
            for image in range(images):
                value = piece[image * PAD : (image + 1) * PAD, cols].astype(f32)
                flat[pl.ds((idx[j] * images + image) * SEQ, SEQ), :] = value[:SEQ]
        out[:, cols] = flat[...].astype(out.dtype)
        return 0

    lax.fori_loop(0, out.shape[1] // LANES, some_columns, 0)


def join_kernel(size, idx, *refs):
    pieces, out = refs[:size], refs[size]
    rows = pieces[0].shape[0]
    for j, piece in enumerate(pieces):
        out[pl.ds(pl.multiple_of(idx[j] * rows, rows), rows), :] = piece[...]


def weight_grad_kernel(idx, left_one, right_one, left_two, right_two, out):
    first = right_one.shape[1]
    out[:, :first] = dot_tn(left_one[...], right_one[...]).astype(bf16)
    out[:, first:] = dot_tn(left_two[...], right_two[...]).astype(bf16)


def split_grad_kernel(part, cut, idx, left_one, right_one, left_two, right_two, tail, *outs):
    i = pl.program_id(0)
    value = jnp.concatenate(
        [
            dot_tn(left_one[...], right_one[...]).astype(bf16),
            dot_tn(left_two[...], right_two[...]).astype(bf16),
            tail[...],
        ],
        axis=1,
    )
    blocks = value.shape[0] // part
    for block in range(blocks):
        at = pl.ds(pl.multiple_of((i * (blocks // 2) + block // 2) * part, part), part)
        rows = value[block * part : (block + 1) * part]
        for given in range(2):

            @pl.when((idx[0] == block % 2) != bool(given))
            def _():
                outs[given][at, :] = rows[:, :cut]
                outs[2 + given][at, :] = rows[:, cut:]


def adam_values(param, first, second, grad, decay):
    scaled = grad / loss_scale
    first = first_decay * first + (1.0 - first_decay) * scaled
    second = second_decay * second + (1.0 - second_decay) * scaled * scaled
    corrected = (
        first
        / (1.0 - first_decay**step_count)
        / (jnp.sqrt(second / (1.0 - second_decay**step_count)) + adam_eps)
    )
    return param - rate * (corrected + decay * param), first, second


def adam_kernel(idx, grad, turned_grad, param, moments, turned, turned_moments, *outs):
    for turn, (g, p, m) in enumerate(((grad, param, moments), (turned_grad, turned, turned_moments))):
        share_out, new_out, mom_out = outs[3 * turn : 3 * turn + 3]
        value = g[...].astype(f32)
        value = value.T if turn else value.reshape(p.shape)
        share_out[...] = value
        new, first, second = adam_values(p[...], m[0], m[1], value, weight_decay)
        new_out[...] = new
        mom_out[0] = first
        mom_out[1] = second


def call(kernel, grid, idx, in_specs, out_specs, out_shapes, args, aliases=None, scratch=(), us=5):
    return pl.pallas_call(
        kernel,
        grid_spec=pltpu.PrefetchScalarGridSpec(
            num_scalar_prefetch=1,
            grid=grid,
            in_specs=in_specs,
            out_specs=out_specs,
            scratch_shapes=list(scratch),
        ),
        out_shape=out_shapes,
        input_output_aliases=aliases or {},
        compiler_params=PARAMS,
        cost_estimate=pl.CostEstimate(flops=us * 10**9, bytes_accessed=us * 3 * 10**6, transcendentals=0),
    )(idx, *args)


def sds(shape, dtype):
    return jax.ShapeDtypeStruct(shape, dtype)


def far_sds(shape, dtype):
    return pltpu.HBM(shape, dtype)


def out_there(value):
    return pltpu.with_memory_space_constraint(value, pltpu.HBM)


def shared_args(buffers, n_args):
    specs = [pl.BlockSpec(memory_space=pl.ANY)] * len(buffers)
    aliases = {1 + n_args + j: j for j in range(len(buffers))}
    return specs, list(buffers), aliases


def attn_fwd(idx, tok, w, vec, bias, buffers):
    nq, (quarters, rows, d), width = idx.shape[0], tok.shape, bias.shape[1]
    specs, extra, aliases = shared_args(buffers, 4)
    out = call(
        functools.partial(attn_fwd_kernel, width, len(buffers)),
        (nq,),
        idx,
        [picked((rows, d)), whole(w.shape), whole(vec.shape), whole(bias.shape)] + specs,
        [picked((rows, d)), picked((rows, 3 * width)), picked((rows, width))] + [whole((rows, d))] * nq,
        [far_sds((quarters, rows, n), bf16) for n in (d, 3 * width, width)] + [sds((rows, d), bf16)] * nq,
        [out_there(tok), w, vec, bias] + extra,
        aliases,
        us=12,
    )
    return out[:3], out[3:]


def ffn(idx, pieces, cot, w, bias, buffers):
    nq, (quarters, rows, d), width = idx.shape[0], cot.shape, bias.shape[1]
    specs, extra, aliases = shared_args(buffers, nq + 3)
    out = call(
        functools.partial(ffn_kernel, nq, len(buffers)),
        (nq,),
        idx,
        [whole((rows, d))] * nq + [picked((rows, d)), whole(w.shape), whole(bias.shape)] + specs,
        [picked((rows, d)), picked((rows, width)), picked((rows, width)), whole((8, width))]
        + [whole((rows, d))] * (2 * nq),
        [far_sds((quarters, rows, n), bf16) for n in (d, width, width)]
        + [sds((8, width), f32)]
        + [sds((rows, d), bf16)] * (2 * nq),
        list(pieces) + [out_there(cot), w, bias] + extra,
        aliases,
        [pltpu.VMEM((rows, d), bf16)],
        us=16,
    )
    return out[:3], out[3][0], out[4 : 4 + nq], out[4 + nq :]


def attn_bwd(idx, pieces, tok, qkv, w, buffers):
    nq, (quarters, rows, d), width = idx.shape[0], tok.shape, qkv.shape[2] // 3
    specs, extra, aliases = shared_args(buffers, nq + 3)
    out = call(
        functools.partial(attn_bwd_kernel, nq, width, len(buffers)),
        (nq,),
        idx,
        [whole((rows, d))] * nq + [picked((rows, d)), picked((rows, 3 * width)), whole(w.shape)] + specs,
        [picked((rows, d)), picked((rows, 3 * width)), whole((8, 3 * width)), whole((8, d))]
        + [whole((rows, d))] * nq,
        [far_sds((quarters, rows, d), bf16), far_sds((quarters, rows, 3 * width), bf16)]
        + [sds((8, 3 * width), f32), sds((8, d), f32)]
        + [sds((rows, d), bf16)] * nq,
        list(pieces) + [out_there(tok), out_there(qkv), w] + extra,
        aliases,
        [pltpu.VMEM((rows, d), bf16), pltpu.VMEM((rows, width), bf16)],
        us=16,
    )
    return out[:2], out[2][0], out[3][:2], out[4:]


def rowwise(kernel, idx, args, kinds, outs):
    rows, d = outs[0].shape
    steps = rows // PAD
    specs = {
        "q": lambda v: pl.BlockSpec((1, PAD, d), lambda i, idx: (idx[0], i, 0)),
        "r": lambda v: pl.BlockSpec((PAD, d), lambda i, idx: (i, 0)),
        "w": lambda v: whole(v.shape),
    }
    return call(
        kernel,
        (steps,),
        idx,
        [specs[kind.lower()](v) for kind, v in zip(kinds, args)],
        [specs["w" if o.shape[0] == 8 else "r"](o) for o in outs],
        outs,
        [out_there(v) if kind in "qR" else v for kind, v in zip(kinds, args)],
        us=3,
    )


def weight_grads(idx, left_one, right_one, left_two, right_two, tail=None, part=None, cut=None):
    d = left_one.shape[2]
    flat = [out_there(v.reshape(-1, v.shape[2])) for v in (left_one, right_one, left_two, right_two)]
    first, second = flat[1].shape[1], flat[3].shape[1]
    step = 256
    n = flat[0].shape[0]
    column = pl.BlockSpec((n, step), lambda i, idx: (0, i))
    specs = [column, whole((n, first)), column, whole((n, second))]
    if tail is None:
        return call(
            weight_grad_kernel,
            (d // step,),
            idx,
            specs,
            pl.BlockSpec((step, first + second), lambda i, idx: (i, 0)),
            sds((d, first + second), bf16),
            flat,
            us=14,
        )
    shapes = [(d // 2, cut)] * 2 + [(d // 2, first + second + tail.shape[1] - cut)] * 2
    return call(
        functools.partial(split_grad_kernel, part, cut),
        (d // step,),
        idx,
        specs + [pl.BlockSpec((step, tail.shape[1]), lambda i, idx: (i, 0))],
        [whole(shape) for shape in shapes],
        [sds(shape, bf16) for shape in shapes],
        flat + [tail],
        us=10,
    )


def adam_pair(idx, grad, turned_grad, param, moments, turned, turned_moments):
    args = [grad, turned_grad, param, moments, turned, turned_moments]
    outs = [sds(v.shape, f32) for v in (param, param, moments, turned, turned, turned_moments)]
    return call(
        adam_kernel, (1,), idx, [whole(v.shape) for v in args], [whole(o.shape) for o in outs], outs, args, us=6
    )


def spread(idx, pieces, dtype):
    rows, d = pieces[0].shape
    total = len(pieces) * rows // PAD * SEQ
    step = d // 2
    return call(
        functools.partial(spread_kernel, len(pieces)),
        (d // step,),
        idx,
        [pl.BlockSpec((rows, step), lambda i, idx: (0, i))] * len(pieces),
        pl.BlockSpec((total, step), lambda i, idx: (0, i)),
        sds((total, d), dtype),
        list(pieces),
        scratch=[pltpu.VMEM((total, LANES), f32)],
        us=4,
    )


def swap(value, flip, size):
    return lax.ppermute(value, TENSOR, [(k, k ^ flip) for k in range(size)])


def add_low(left, right):
    return (left.astype(f32) + right.astype(f32)).astype(bf16)


def tie(value, *after):
    return lax.optimization_barrier((value,) + after)[0]


def shard_swap(value, flip, size):
    return lax.ppermute(value, SHARD, [(k, k ^ flip) for k in range(size)])


def gather_shards(value, size):
    outer = [value] + [shard_swap(value, 2 * k, size) for k in range(1, size // 2)]
    pieces = []
    for piece in outer:
        pieces += [piece, shard_swap(piece, 1, size)]
    rows, columns = value.shape
    index = jnp.arange(size, dtype=jnp.int32) ^ lax.axis_index(SHARD).astype(jnp.int32)
    return call(
        functools.partial(join_kernel, size),
        (1,),
        index,
        [whole(value.shape)] * size,
        whole((size * rows, columns)),
        sds((size * rows, columns), value.dtype),
        pieces,
        us=3,
    ), outer[1]


def scatter_outer(kept, given, size):
    me = lax.axis_index(SHARD) // 2
    take = lambda array, at: lax.dynamic_index_in_dim(array, at, 0, keepdims=False)
    value = add_low(kept, given).reshape(size // 2, -1, kept.shape[1])
    return value, [take(value, me)] + [shard_swap(take(value, me ^ k), 2 * k, size) for k in range(1, size // 2)]


def add_all(values):
    return functools.reduce(jnp.add, [value.astype(f32) for value in values])


def adamw(param, moments, grad, decay):
    scaled = grad / loss_scale
    first = first_decay * moments[0] + (1.0 - first_decay) * scaled
    second = second_decay * moments[1] + (1.0 - second_decay) * scaled * scaled
    corrected = (
        first
        / (1.0 - first_decay**step_count)
        / (jnp.sqrt(second / (1.0 - second_decay**step_count)) + adam_eps)
    )
    return (param - rate * (corrected + decay * param), jnp.stack([first, second]))


def on_device(
    n_shard,
    n_tensor,
    tokens,
    cotangent,
    input_weight,
    input_moments,
    input_bias,
    input_bias_moments,
    output_weight,
    output_moments,
    expand_weight,
    expand_moments,
    expand_bias,
    expand_bias_moments,
    shrink_weight,
    shrink_moments,
    vectors,
    vector_moments,
):
    rows, d = tokens.shape
    images = rows // SEQ
    per = images // n_tensor
    part = d // n_shard
    width = input_weight.shape[2]
    hidden = expand_weight.shape[1]
    me = lax.axis_index(TENSOR).astype(jnp.int32)
    index = jnp.arange(n_tensor, dtype=jnp.int32) ^ me
    near, far, own = index[:2], index[2:], index[:1]

    small = jnp.concatenate([vectors, expand_bias.reshape(1, -1)], axis=0)
    small = jnp.pad(small, ((0, 0), (0, LANES - part)))
    bias_rows = jnp.pad(input_bias, ((0, 0), (0, LANES - input_bias.shape[1])))
    small = jnp.concatenate([small, bias_rows], axis=0)
    n_small = small.shape[0]
    small = jnp.pad(small, ((0, part - n_small), (0, 0)))
    pack_one = jnp.concatenate(
        [input_weight[c] for c in range(3)] + [output_weight.T, small], axis=1
    ).astype(bf16)
    pack_two = jnp.concatenate([expand_weight, shrink_weight.T], axis=1).astype(bf16)
    w_one, first = gather_shards(pack_one, n_shard)
    w_two = lax.all_gather(tie(pack_two, first), SHARD, axis=0, tiled=True)
    small = w_one[:, 4 * width :].reshape(n_shard, part, LANES)[:, :n_small].astype(f32)
    vec = jnp.pad(small[:, :6, :part].transpose(1, 0, 2).reshape(6, d), ((0, 2), (0, 0)))
    full_expand_bias = small[:, 6, :part].reshape(1, hidden)
    full_bias = small[:, 7:9, : width // n_shard].transpose(1, 0, 2).reshape(2, width)

    def padded(values):
        values = values.reshape(images, SEQ, d)
        values = jnp.pad(values, ((0, 0), (0, PAD - SEQ), (0, 0)))
        return values.reshape(n_tensor, per * PAD, d)

    tok, cot = padded(tokens), padded(cotangent)
    far = tie(far, cot)
    q_rows = per * PAD
    block = (q_rows, d)

    buffers, (p2, p3) = attn_fwd(far, tok, w_one, vec, full_bias, ())
    sum2 = add_low(p2, swap(p3, 1, n_tensor))
    cross = swap(sum2, 2, n_tensor)
    (inputs_all, qkv_all, ctx_all), (p0, p1) = attn_fwd(tie(near, sum2), tok, w_one, vec, full_bias, buffers)
    sum0 = add_low(p0, swap(p1, 1, n_tensor))
    attended, normed = rowwise(
        mid_kernel, own, [tok, sum0, cross, vec], "qrrw", [far_sds(block, f32), sds(block, bf16)]
    )

    def gather_rows(value):
        return (value, swap(value, 1, n_tensor)), swap(value, 2, n_tensor)

    def gather_far(over, *after):
        over = tie(over, *after)
        return over, swap(over, 1, n_tensor)

    near_x, over_x = gather_rows(normed)
    buffers, bias_near, shrink_near, mid_near = ffn(near, near_x, cot, w_two, full_expand_bias, ())
    far_x = gather_far(over_x, mid_near[0])
    ffn_all, bias_far, shrink_far, mid_far = ffn(far, far_x, cot, w_two, full_expand_bias, buffers)
    x_all, hid_all, pre_all = ffn_all

    def scatter_rows(near_parts, far_parts):
        over = add_low(far_parts[0], swap(far_parts[1], 1, n_tensor))
        return add_low(near_parts[0], swap(near_parts[1], 1, n_tensor)), over

    mid_mine, mid_over = scatter_rows(mid_near, mid_far)
    mid_theirs = swap(mid_over, 2, n_tensor)
    grads_two = weight_grads(tie(own, mid_over), x_all, pre_all, cot, hid_all)
    share_two = lax.psum_scatter(grads_two, SHARD, scatter_dimension=0, tiled=True)
    mid_theirs = tie(mid_theirs, grads_two)
    mid, mid_low, vec_mid = rowwise(
        mid_back_kernel,
        own,
        [attended, cot, mid_mine, mid_theirs, vec],
        "Rqrrw",
        [far_sds(block, f32), sds(block, bf16), sds((8, d), f32)],
    )

    near_m, over_m = gather_rows(mid_low)
    buffers, sums_near, vec_near, part_near = attn_bwd(near, near_m, tok, qkv_all, w_one, ())
    far_m = gather_far(over_m, part_near[0])
    shrink_mine, shrink_over = scatter_rows(shrink_near, shrink_far)
    shrink_theirs = swap(tie(shrink_over, part_near[0]), 2, n_tensor)
    (mid_all, grad_all), sums_far, vec_far, part_far = attn_bwd(far, far_m, tok, qkv_all, w_one, buffers)

    mine, over = scatter_rows(part_near, part_far)
    theirs = swap(over, 2, n_tensor)

    vec_grads = jnp.concatenate([vec_near + vec_far, vec_mid[:4], (bias_near + bias_far).reshape(1, d)])
    vec_grads = vec_grads.reshape(7, n_shard, part).transpose(1, 0, 2)
    vec_grads = jnp.pad(vec_grads, ((0, 0), (0, 0), (0, LANES - part)))
    sums = sums_near + sums_far
    bias_grads = jnp.stack([sums[:width], sums[2 * width :]]).reshape(2, n_shard, -1).transpose(1, 0, 2)
    bias_grads = jnp.pad(bias_grads, ((0, 0), (0, 0), (0, LANES - bias_grads.shape[2])))
    tail = jnp.concatenate([vec_grads, bias_grads], axis=1)
    tail = jnp.pad(tail, ((0, 0), (0, part - n_small), (0, 0))).reshape(d, LANES).astype(bf16)
    grads_one = weight_grads(
        tie(lax.axis_index(SHARD).astype(jnp.int32).reshape(1) % 2, over),
        inputs_all,
        grad_all,
        mid_all,
        ctx_all,
        tail,
        part,
        2 * width,
    )
    halves = [(kept, shard_swap(given, 1, n_shard)) for kept, given in (grads_one[:2], grads_one[2:])]

    theirs = tie(theirs, grads_one[0])
    (token_low,) = rowwise(token_back_kernel, own, [tok, mid, mine, theirs, vec], "qRrrw", [sds(block, bf16)])
    (kept_one, given_one), (kept_two, given_two) = halves
    half_one = scatter_outer(kept_one, tie(given_one, token_low), n_shard)
    halves = [half_one, scatter_outer(kept_two, tie(given_two, half_one[0]), n_shard)]
    result = attended + (shrink_mine.astype(f32) + shrink_theirs.astype(f32)) + vec[5]
    near_o, over_o = gather_rows(tie(result.astype(bf16), theirs))
    near_t, over_t = gather_rows(token_low)

    share_two = tie(share_two, *[half[0] for half in halves])
    share_expand, new_expand, mom_expand, share_shrink, new_shrink, mom_shrink = adam_pair(
        own, share_two[:, :hidden], share_two[:, hidden:], expand_weight, expand_moments, shrink_weight, shrink_moments
    )
    token_gradient = spread(index, near_t + gather_far(over_t, share_expand), f32)
    share_one, share_rest = [add_all([tie(half[1][0], token_gradient)] + half[1][1:]) for half in halves]
    small = share_rest[:n_small, 2 * width :]
    share_vectors = small[:6, :part]
    share_vectors = share_vectors + swap(share_vectors, 1, n_tensor)
    share_vectors = share_vectors + swap(share_vectors, 2, n_tensor)
    share_expand_bias = small[6, :part]
    share_bias = small[7:9, : width // n_shard]

    columns = jnp.concatenate([share_one, share_rest[:, :width]], axis=1)
    share_input, new_input, mom_input, share_output, new_output, mom_output = adam_pair(
        own,
        columns.reshape(part, 3, width).transpose(1, 0, 2),
        share_rest[:, width : 2 * width],
        input_weight,
        input_moments,
        output_weight,
        output_moments,
    )
    block_output = spread(index, near_o + gather_far(over_o, share_input), bf16)
    new_bias, mom_bias = adamw(input_bias, input_bias_moments, share_bias, 0.0)
    new_expand_bias, mom_expand_bias = adamw(
        expand_bias, expand_bias_moments, share_expand_bias, 0.0
    )
    new_vectors, mom_vectors = adamw(vectors, vector_moments, share_vectors, 0.0)
    return (
        block_output,
        token_gradient,
        share_input,
        share_bias,
        share_output,
        share_expand,
        share_expand_bias,
        share_shrink,
        share_vectors,
        new_input,
        new_bias,
        new_output,
        new_expand,
        new_expand_bias,
        new_shrink,
        new_vectors,
        mom_input,
        mom_bias,
        mom_output,
        mom_expand,
        mom_expand_bias,
        mom_shrink,
        mom_vectors,
    )


def solution(mesh):
    def body(*args):
        return on_device(mesh.shape[SHARD], mesh.shape[TENSOR], *args)

    return jax.shard_map(
        body,
        mesh=mesh,
        in_specs=(
            P(SHARD, None),
            P(SHARD, None),
            P(None, SHARD, TENSOR),
            P(None, None, SHARD, TENSOR),
            P(None, (TENSOR, SHARD)),
            P(None, None, (TENSOR, SHARD)),
            P(TENSOR, SHARD),
            P(None, TENSOR, SHARD),
            P(SHARD, TENSOR),
            P(None, SHARD, TENSOR),
            P((TENSOR, SHARD)),
            P(None, (TENSOR, SHARD)),
            P(TENSOR, SHARD),
            P(None, TENSOR, SHARD),
            P(None, SHARD),
            P(None, None, SHARD),
        ),
        out_specs=(
            P(SHARD, None),
            P(SHARD, None),
            P(None, SHARD, TENSOR),
            P(None, (TENSOR, SHARD)),
            P(TENSOR, SHARD),
            P(SHARD, TENSOR),
            P((TENSOR, SHARD)),
            P(TENSOR, SHARD),
            P(None, SHARD),
            P(None, SHARD, TENSOR),
            P(None, (TENSOR, SHARD)),
            P(TENSOR, SHARD),
            P(SHARD, TENSOR),
            P((TENSOR, SHARD)),
            P(TENSOR, SHARD),
            P(None, SHARD),
            P(None, None, SHARD, TENSOR),
            P(None, None, (TENSOR, SHARD)),
            P(None, TENSOR, SHARD),
            P(None, SHARD, TENSOR),
            P(None, (TENSOR, SHARD)),
            P(None, TENSOR, SHARD),
            P(None, None, SHARD),
        ),
        check_vma=False,
    )
```

```python
import functools

import jax
import jax.numpy as jnp
from jax import lax
from jax.experimental import pallas as pl
from jax.experimental.pallas import tpu as pltpu
from jax.sharding import PartitionSpec as P


HEAD = 64
SEQ = 197
PAD = 208
LANES = 128
SHARD, TENSOR = "shard", "tensor"

norm_eps = 1e-06
rate = 0.003
first_decay = 0.9
second_decay = 0.95
weight_decay = 0.05
step_count = 2.0
adam_eps = 1e-08
loss_scale = 128.0


bf16 = jnp.bfloat16
f32 = jnp.float32
NT = (((1,), (1,)), ((), ()))
TN = (((0,), (0,)), ((), ()))
PARAMS = pltpu.CompilerParams(vmem_limit_bytes=40 * 1024 * 1024)


def dot(left, right):
    return jnp.dot(left, right, preferred_element_type=f32)


def dot_nt(left, right):
    return lax.dot_general(left, right, NT, preferred_element_type=f32)


def dot_tn(left, right):
    return lax.dot_general(left, right, TN, preferred_element_type=f32)


def whole(shape):
    return pl.BlockSpec(shape, lambda i, idx: (0,) * len(shape))


def picked(shape):
    return pl.BlockSpec((1,) + shape, lambda i, idx: (idx[i],) + (0,) * len(shape))


def store_one(refs, i, value):
    for j, ref in enumerate(refs):

        @pl.when(i == j)
        def _():
            ref[...] = value


def load_one(refs, i, scratch):
    for j, ref in enumerate(refs):

        @pl.when(i == j)
        def _():
            scratch[...] = ref[...]

    return scratch[...]


def norm_stats(values):
    centred = values - jnp.mean(values, axis=-1, keepdims=True)
    spread = jnp.mean(centred * centred, axis=-1, keepdims=True)
    inverse = lax.rsqrt(spread + norm_eps)
    return centred * inverse, inverse


def norm_back(unit, inverse, grad, gain):
    scaled = grad * gain
    mean_one = jnp.mean(scaled, axis=-1, keepdims=True)
    mean_two = jnp.mean(scaled * unit, axis=-1, keepdims=True)
    return inverse * (scaled - mean_one - unit * mean_two)


def attn_fwd_kernel(width, shared, idx, tok, w, vec, bias, *rest):
    rest = rest[shared:]
    inputs_out, qkv_out, ctx_out = rest[:3]
    parts = rest[3:]
    i = pl.program_id(0)
    unit, _ = norm_stats(tok[0].astype(f32))
    inputs = (unit * vec[0:1, :] + vec[1:2, :]).astype(bf16)
    inputs_out[0] = inputs
    project = dot(inputs, w[:, : 3 * width])
    query = (project[:, :width] + bias[0:1, :]).astype(bf16)
    keys = project[:, width : 2 * width].astype(bf16)
    values = (project[:, 2 * width :] + bias[1:2, :]).astype(bf16)
    qkv_out[0, :, :width] = query
    qkv_out[0, :, width : 2 * width] = keys
    qkv_out[0, :, 2 * width :] = values
    scale = bf16(HEAD ** (-0.5))
    lane = lax.broadcasted_iota(jnp.int32, (1, LANES), 1)
    live = lax.broadcasted_iota(jnp.int32, (1, PAD), 1) < SEQ

    def one_image(image, _):
        rows = pl.ds(pl.multiple_of(image * PAD, PAD), PAD)
        for pair in range(width // LANES):
            at = [slice(c * width + pair * LANES, c * width + (pair + 1) * LANES) for c in range(3)]
            q2, k2, v2 = qkv_out[0, rows, at[0]] * scale, qkv_out[0, rows, at[1]], qkv_out[0, rows, at[2]]
            outs = []
            for half in range(LANES // HEAD):
                mine = (lane // HEAD) == half
                scores = dot_nt(jnp.where(mine, q2, bf16(0)), k2)
                scores = jnp.where(live, scores, -1e30)
                raised = jnp.exp(scores - jnp.max(scores, axis=-1, keepdims=True))
                total = jnp.sum(raised, axis=-1, keepdims=True)
                outs.append(dot((raised * (1.0 / total)).astype(bf16), v2))
            ctx_out[0, rows, at[0]] = jnp.where(lane < HEAD, outs[0], outs[1]).astype(bf16)
        return 0

    lax.fori_loop(0, tok.shape[1] // PAD, one_image, 0)
    store_one(parts, i, dot_nt(ctx_out[0], w[:, 3 * width : 4 * width]).astype(bf16))


def ffn_kernel(nq, shared, idx, *refs):
    pieces, (cot, w, bias) = refs[:nq], refs[nq : nq + 3]
    refs = refs[nq + 3 + shared :]
    x_out, hid_out, pre_out, bias_out = refs[:4]
    shrink_parts, mid_parts, scratch = refs[4 : 4 + nq], refs[4 + nq : 4 + 2 * nq], refs[-1]
    i = pl.program_id(0)
    width = bias.shape[1]
    x = load_one(pieces, i, scratch)
    x_out[0] = x
    back = cot[0]

    @pl.when(i == 0)
    def _():
        bias_out[...] = jnp.zeros_like(bias_out)

    step = 512

    def some_columns(k, _):
        start = pl.multiple_of(k * step, step)
        cols, second = pl.ds(start, step), pl.ds(width + start, step)
        pre = dot(x, w[:, cols]) + bias[0:1, cols]
        grad = dot(back, w[:, second])
        share = 0.5 + 0.5 * lax.erf(pre * (0.5**0.5))
        slope = share + pre * (jnp.exp(-0.5 * pre * pre) * 0.3989422804014327)
        hid_out[0, :, cols] = (pre * share).astype(bf16)
        pre_grad = (slope * grad).astype(bf16)
        pre_out[0, :, cols] = pre_grad
        bias_out[0:1, cols] += jnp.sum(pre_grad.astype(f32), axis=0, keepdims=True)
        return 0

    lax.fori_loop(0, width // step, some_columns, 0)

    def some_outputs(k, _):
        at = pl.ds(pl.multiple_of(k * step, step), step)
        for ref, value, start in ((shrink_parts, hid_out, width), (mid_parts, pre_out, 0)):
            part = dot_nt(value[0], w[at, start : start + width]).astype(bf16)
            for j in range(nq):

                @pl.when(i == j)
                def _():
                    ref[j][:, at] = part

        return 0

    lax.fori_loop(0, x.shape[1] // step, some_outputs, 0)


def attn_bwd_kernel(nq, width, shared, idx, *refs):
    pieces, (tok, qkv, w) = refs[:nq], refs[nq : nq + 3]
    refs = refs[nq + 3 + shared :]
    mid_out, grad_out, sums_out, vec_out = refs[:4]
    parts, scratch, ctx_grads = refs[4 : 4 + nq], refs[-2], refs[-1]
    i = pl.program_id(0)
    mid = load_one(pieces, i, scratch)
    mid_out[0] = mid
    ctx_grad = dot(mid, w[:, 3 * width : 4 * width]).astype(bf16)
    scale = bf16(HEAD ** (-0.5))
    lane = lax.broadcasted_iota(jnp.int32, (1, LANES), 1)
    live = lax.broadcasted_iota(jnp.int32, (PAD, 1), 0) < SEQ

    ctx_grads[...] = ctx_grad

    pairs = width // LANES

    def one_pair(step, _):
        rows = pl.ds(pl.multiple_of(step // pairs * PAD, PAD), PAD)
        start = step % pairs * LANES
        at = [pl.ds(pl.multiple_of(c * width + start, LANES), LANES) for c in range(3)]
        q2, k2, v2 = qkv[0, rows, at[0]] * scale, qkv[0, rows, at[1]], qkv[0, rows, at[2]]
        c2 = ctx_grads[rows, at[0]]
        outs = []
        for half in range(LANES // HEAD):
            mine = (lane // HEAD) == half
            scores = dot_nt(k2, jnp.where(mine, q2, bf16(0)))
            scores = jnp.where(live, scores, -1e30)
            raised = jnp.exp(scores - jnp.max(scores, axis=0, keepdims=True))
            prob = raised * (1.0 / jnp.sum(raised, axis=0, keepdims=True))
            prob_grad = dot_nt(v2, jnp.where(mine, c2, bf16(0)))
            row_dot = jnp.sum(prob_grad * prob, axis=0, keepdims=True)
            score_grad = (prob * (prob_grad - row_dot)).astype(bf16)
            outs.append(
                (
                    dot_tn(score_grad, k2) * HEAD ** (-0.5),
                    dot(score_grad, q2),
                    dot(prob.astype(bf16), c2),
                )
            )
        for c in range(3):
            grad_out[0, rows, at[c]] = jnp.where(lane < HEAD, outs[0][c], outs[1][c]).astype(bf16)
        return 0

    lax.fori_loop(0, tok.shape[1] // PAD * pairs, one_pair, 0)
    grads = grad_out[0]
    part = dot_nt(grads, w[:, : 3 * width])
    store_one(parts, i, part.astype(bf16))
    unit, _ = norm_stats(tok[0].astype(f32))

    @pl.when(i == 0)
    def _():
        sums_out[...] = jnp.zeros_like(sums_out)
        vec_out[...] = jnp.zeros_like(vec_out)

    sums_out[0:1, :] += jnp.sum(grads.astype(f32), axis=0, keepdims=True)
    vec_out[0:1, :] += jnp.sum(part * unit, axis=0, keepdims=True)
    vec_out[1:2, :] += jnp.sum(part, axis=0, keepdims=True)


def mid_kernel(idx, tok, mine, theirs, vec, attended_out, normed_out):
    attended = tok[0].astype(f32) + (mine[...].astype(f32) + theirs[...].astype(f32)) + vec[2:3, :]
    attended_out[...] = attended
    unit, _ = norm_stats(attended)
    normed_out[...] = (unit * vec[3:4, :] + vec[4:5, :]).astype(bf16)


def mid_back_kernel(idx, attended, cot, mine, theirs, vec, mid_out, low_out, sums_out):
    grad = mine[...].astype(f32) + theirs[...].astype(f32)
    unit, inverse = norm_stats(attended[...])
    back = cot[0].astype(f32)
    mid = back + norm_back(unit, inverse, grad, vec[3:4, :])
    mid_out[...] = mid
    low_out[...] = mid.astype(bf16)

    @pl.when(pl.program_id(0) == 0)
    def _():
        sums_out[...] = jnp.zeros_like(sums_out)

    sums_out[0:1, :] += jnp.sum(mid, axis=0, keepdims=True)
    sums_out[1:2, :] += jnp.sum(grad * unit, axis=0, keepdims=True)
    sums_out[2:3, :] += jnp.sum(grad, axis=0, keepdims=True)
    sums_out[3:4, :] += jnp.sum(back, axis=0, keepdims=True)


def token_back_kernel(idx, tok, mid, mine, theirs, vec, out):
    grad = mine[...].astype(f32) + theirs[...].astype(f32)
    unit, inverse = norm_stats(tok[0].astype(f32))
    out[...] = (mid[...] + norm_back(unit, inverse, grad, vec[0:1, :])).astype(bf16)


def spread_kernel(nq, idx, *refs):
    pieces, out, flat = refs[:nq], refs[nq], refs[nq + 1]

    def some_columns(k, _):
        cols = pl.ds(pl.multiple_of(k * LANES, LANES), LANES)
        for j, piece in enumerate(pieces):
            images = piece.shape[0] // PAD
            for image in range(images):
                value = piece[image * PAD : (image + 1) * PAD, cols].astype(f32)
                flat[pl.ds((idx[j] * images + image) * SEQ, SEQ), :] = value[:SEQ]
        out[:, cols] = flat[...].astype(out.dtype)
        return 0

    lax.fori_loop(0, out.shape[1] // LANES, some_columns, 0)


def join_kernel(size, idx, *refs):
    pieces, out = refs[:size], refs[size]
    rows = pieces[0].shape[0]
    for j, piece in enumerate(pieces):
        out[pl.ds(pl.multiple_of(idx[j] * rows, rows), rows), :] = piece[...]


def weight_grad_kernel(idx, left_one, right_one, left_two, right_two, out):
    first = right_one.shape[1]
    out[:, :first] = dot_tn(left_one[...], right_one[...]).astype(bf16)
    out[:, first:] = dot_tn(left_two[...], right_two[...]).astype(bf16)


def split_grad_kernel(part, cut, idx, left_one, right_one, left_two, right_two, tail, *outs):
    i = pl.program_id(0)
    value = jnp.concatenate(
        [
            dot_tn(left_one[...], right_one[...]).astype(bf16),
            dot_tn(left_two[...], right_two[...]).astype(bf16),
            tail[...],
        ],
        axis=1,
    )
    blocks = value.shape[0] // part
    for block in range(blocks):
        at = pl.ds(pl.multiple_of((i * (blocks // 2) + block // 2) * part, part), part)
        rows = value[block * part : (block + 1) * part]
        for given in range(2):

            @pl.when((idx[0] == block % 2) != bool(given))
            def _():
                outs[given][at, :] = rows[:, :cut]
                outs[2 + given][at, :] = rows[:, cut:]


def adam_values(param, first, second, grad, decay):
    scaled = grad / loss_scale
    first = first_decay * first + (1.0 - first_decay) * scaled
    second = second_decay * second + (1.0 - second_decay) * scaled * scaled
    corrected = (
        first
        / (1.0 - first_decay**step_count)
        / (jnp.sqrt(second / (1.0 - second_decay**step_count)) + adam_eps)
    )
    return param - rate * (corrected + decay * param), first, second


def adam_store(value, p, m, share_out, new_out, mom_out):
    share_out[...] = value
    new_out[...], mom_out[0], mom_out[1] = adam_values(p[...], m[0], m[1], value, weight_decay)


def adam_hidden_kernel(idx, grad, turned_grad, param, moments, turned, turned_moments, *outs):
    adam_store(grad[...].astype(f32), param, moments, *outs[:3])
    adam_store(turned_grad[...].astype(f32).T, turned, turned_moments, *outs[3:])


def adam_attention_kernel(n, idx, *refs):
    first, second, (param, moments, turned, turned_moments), outs = refs[:n], refs[n : 2 * n], refs[2 * n : 2 * n + 4], refs[2 * n + 4 :]
    one = functools.reduce(jnp.add, [ref[...].astype(f32) for ref in first])
    two = functools.reduce(jnp.add, [ref[...].astype(f32) for ref in second])
    width = param.shape[2]
    for c, value in enumerate((one[:, :width], one[:, width:], two[:, :width])):
        adam_store(value, param.at[c], moments.at[:, c], outs[0].at[c], outs[1].at[c], outs[2].at[:, c])
    adam_store(two[:, width : 2 * width].T, turned, turned_moments, *outs[3:6])
    outs[6][...] = two[:, 2 * width :]


def sum_kernel(idx, kept, given, *outs):
    rows = outs[0].shape[0]
    for k, out in enumerate(outs):
        at = pl.ds(pl.multiple_of((idx[0] ^ k) * rows, rows), rows)
        out[...] = (kept[at, :].astype(f32) + given[at, :].astype(f32)).astype(bf16)


def pad_kernel(idx, values, out, flat):
    rows = values.shape[0]
    live = lax.broadcasted_iota(jnp.int32, (PAD, 1), 0) < SEQ
    per = out.shape[1] // PAD

    def some_columns(k, _):
        cols = pl.ds(pl.multiple_of(k * LANES, LANES), LANES)
        flat[:rows, :] = values[:, cols].astype(f32)
        for image in range(rows // SEQ):
            value = jnp.where(live, flat[image * SEQ : image * SEQ + PAD, :], 0.0)
            at = slice(image % per * PAD, (image % per + 1) * PAD)
            out[image // per, at, cols] = value.astype(bf16)
        return 0

    lax.fori_loop(0, values.shape[1] // LANES, some_columns, 0)


def pack_kernel(idx, inner, outer, vectors, hidden_bias, bias, out, small):
    part, width = inner.shape[1:]
    for c in range(3):
        out[:, c * width : (c + 1) * width] = inner[c].astype(bf16)
    out[:, 3 * width : 4 * width] = outer[...].T.astype(bf16)
    small[...] = jnp.zeros_like(small)
    small[0:6, :part] = vectors[...]
    small[6:7, :part] = hidden_bias[...]
    small[7:9, : bias.shape[1]] = bias[...]
    out[:, 4 * width :] = small[...].astype(bf16)


def call(kernel, grid, idx, in_specs, out_specs, out_shapes, args, aliases=None, scratch=(), us=5):
    return pl.pallas_call(
        kernel,
        grid_spec=pltpu.PrefetchScalarGridSpec(
            num_scalar_prefetch=1,
            grid=grid,
            in_specs=in_specs,
            out_specs=out_specs,
            scratch_shapes=list(scratch),
        ),
        out_shape=out_shapes,
        input_output_aliases=aliases or {},
        compiler_params=PARAMS,
        cost_estimate=pl.CostEstimate(flops=us * 10**9, bytes_accessed=us * 3 * 10**6, transcendentals=0),
    )(idx, *args)


def sds(shape, dtype):
    return jax.ShapeDtypeStruct(shape, dtype)


def far_sds(shape, dtype):
    return pltpu.HBM(shape, dtype)


def out_there(value):
    return pltpu.with_memory_space_constraint(value, pltpu.HBM)


def shared_args(buffers, n_args):
    specs = [pl.BlockSpec(memory_space=pl.ANY)] * len(buffers)
    aliases = {1 + n_args + j: j for j in range(len(buffers))}
    return specs, list(buffers), aliases


def attn_fwd(idx, tok, w, vec, bias, buffers):
    nq, (quarters, rows, d), width = idx.shape[0], tok.shape, bias.shape[1]
    specs, extra, aliases = shared_args(buffers, 4)
    out = call(
        functools.partial(attn_fwd_kernel, width, len(buffers)),
        (nq,),
        idx,
        [picked((rows, d)), whole(w.shape), whole(vec.shape), whole(bias.shape)] + specs,
        [picked((rows, d)), picked((rows, 3 * width)), picked((rows, width))] + [whole((rows, d))] * nq,
        [far_sds((quarters, rows, n), bf16) for n in (d, 3 * width, width)] + [sds((rows, d), bf16)] * nq,
        [out_there(tok), w, vec, bias] + extra,
        aliases,
        us=12,
    )
    return out[:3], out[3:]


def ffn(idx, pieces, cot, w, bias, buffers):
    nq, (quarters, rows, d), width = idx.shape[0], cot.shape, bias.shape[1]
    specs, extra, aliases = shared_args(buffers, nq + 3)
    out = call(
        functools.partial(ffn_kernel, nq, len(buffers)),
        (nq,),
        idx,
        [whole((rows, d))] * nq + [picked((rows, d)), whole(w.shape), whole(bias.shape)] + specs,
        [picked((rows, d)), picked((rows, width)), picked((rows, width)), whole((8, width))]
        + [whole((rows, d))] * (2 * nq),
        [far_sds((quarters, rows, n), bf16) for n in (d, width, width)]
        + [sds((8, width), f32)]
        + [sds((rows, d), bf16)] * (2 * nq),
        list(pieces) + [out_there(cot), w, bias] + extra,
        aliases,
        [pltpu.VMEM((rows, d), bf16)],
        us=16,
    )
    return out[:3], out[3][0], out[4 : 4 + nq], out[4 + nq :]


def attn_bwd(idx, pieces, tok, qkv, w, buffers):
    nq, (quarters, rows, d), width = idx.shape[0], tok.shape, qkv.shape[2] // 3
    specs, extra, aliases = shared_args(buffers, nq + 3)
    out = call(
        functools.partial(attn_bwd_kernel, nq, width, len(buffers)),
        (nq,),
        idx,
        [whole((rows, d))] * nq + [picked((rows, d)), picked((rows, 3 * width)), whole(w.shape)] + specs,
        [picked((rows, d)), picked((rows, 3 * width)), whole((8, 3 * width)), whole((8, d))]
        + [whole((rows, d))] * nq,
        [far_sds((quarters, rows, d), bf16), far_sds((quarters, rows, 3 * width), bf16)]
        + [sds((8, 3 * width), f32), sds((8, d), f32)]
        + [sds((rows, d), bf16)] * nq,
        list(pieces) + [out_there(tok), out_there(qkv), w] + extra,
        aliases,
        [pltpu.VMEM((rows, d), bf16), pltpu.VMEM((rows, width), bf16)],
        us=16,
    )
    return out[:2], out[2][0], out[3][:2], out[4:]


def rowwise(kernel, idx, args, kinds, outs):
    rows, d = outs[0].shape
    steps = rows // PAD
    specs = {
        "q": lambda v: pl.BlockSpec((1, PAD, d), lambda i, idx: (idx[0], i, 0)),
        "r": lambda v: pl.BlockSpec((PAD, d), lambda i, idx: (i, 0)),
        "w": lambda v: whole(v.shape),
    }
    return call(
        kernel,
        (steps,),
        idx,
        [specs[kind.lower()](v) for kind, v in zip(kinds, args)],
        [specs["w" if o.shape[0] == 8 else "r"](o) for o in outs],
        outs,
        [out_there(v) if kind in "qR" else v for kind, v in zip(kinds, args)],
        us=3,
    )


def weight_grads(idx, left_one, right_one, left_two, right_two, tail=None, part=None, cut=None):
    d = left_one.shape[2]
    flat = [out_there(v.reshape(-1, v.shape[2])) for v in (left_one, right_one, left_two, right_two)]
    first, second = flat[1].shape[1], flat[3].shape[1]
    step = 256
    n = flat[0].shape[0]
    column = pl.BlockSpec((n, step), lambda i, idx: (0, i))
    specs = [column, whole((n, first)), column, whole((n, second))]
    if tail is None:
        return call(
            weight_grad_kernel,
            (d // step,),
            idx,
            specs,
            pl.BlockSpec((step, first + second), lambda i, idx: (i, 0)),
            sds((d, first + second), bf16),
            flat,
            us=14,
        )
    shapes = [(d // 2, cut)] * 2 + [(d // 2, first + second + tail.shape[1] - cut)] * 2
    return call(
        functools.partial(split_grad_kernel, part, cut),
        (d // step,),
        idx,
        specs + [pl.BlockSpec((step, tail.shape[1]), lambda i, idx: (i, 0))],
        [whole(shape) for shape in shapes],
        [sds(shape, bf16) for shape in shapes],
        flat + [tail],
        us=10,
    )


def adam_hidden(idx, grads, param, moments, turned, turned_moments):
    part, hidden = param.shape
    step = 256
    count = hidden // step
    wide = pl.BlockSpec((part, step), lambda i, idx: (0, i))
    wide_two = pl.BlockSpec((2, part, step), lambda i, idx: (0, 0, i))
    tall = pl.BlockSpec((step, part), lambda i, idx: (i, 0))
    tall_two = pl.BlockSpec((2, step, part), lambda i, idx: (0, i, 0))
    beside = pl.BlockSpec((part, step), lambda i, idx: (0, i + count))
    outs = [sds(v.shape, f32) for v in (param, param, moments, turned, turned, turned_moments)]
    return call(
        adam_hidden_kernel,
        (count,),
        idx,
        [wide, beside, wide, wide_two, tall, tall_two],
        [wide, wide, wide_two, tall, tall, tall_two],
        outs,
        [grads, grads, param, moments, turned, turned_moments],
        us=4,
    )


def adam_attention(idx, first, second, param, moments, turned, turned_moments):
    args = list(first) + list(second) + [param, moments, turned, turned_moments]
    outs = [sds(v.shape, f32) for v in (param, param, moments, turned, turned, turned_moments)]
    outs.append(sds((first[0].shape[0], LANES), f32))
    return call(
        functools.partial(adam_attention_kernel, len(first)),
        (1,),
        idx,
        [whole(v.shape) for v in args],
        [whole(o.shape) for o in outs],
        outs,
        args,
        us=3,
    )


def padded(idx, values, quarters):
    rows, d = values.shape
    images = rows // SEQ
    shape = (quarters, images // quarters * PAD, d)
    step = d // 2
    return call(
        pad_kernel,
        (d // step,),
        idx,
        [pl.BlockSpec((rows, step), lambda i, idx: (0, i))],
        pl.BlockSpec(shape[:2] + (step,), lambda i, idx: (0, 0, i)),
        far_sds(shape, bf16),
        [values],
        scratch=[pltpu.VMEM(((images - 1) * SEQ + PAD + 5, LANES), f32)],
        us=4,
    )


def pack(idx, inner, outer, vectors, hidden_bias, bias):
    part, width = inner.shape[1:]
    args = [inner, outer, vectors, hidden_bias.reshape(1, -1), bias]
    shape = (part, 4 * width + LANES)
    return call(
        pack_kernel,
        (1,),
        idx,
        [whole(v.shape) for v in args],
        whole(shape),
        sds(shape, bf16),
        args,
        scratch=[pltpu.VMEM((part, LANES), f32)],
        us=2,
    )


def spread(idx, pieces, dtype):
    rows, d = pieces[0].shape
    total = len(pieces) * rows // PAD * SEQ
    step = d // 2
    return call(
        functools.partial(spread_kernel, len(pieces)),
        (d // step,),
        idx,
        [pl.BlockSpec((rows, step), lambda i, idx: (0, i))] * len(pieces),
        pl.BlockSpec((total, step), lambda i, idx: (0, i)),
        sds((total, d), dtype),
        list(pieces),
        scratch=[pltpu.VMEM((total, LANES), f32)],
        us=4,
    )


def swap(value, flip, size):
    return lax.ppermute(value, TENSOR, [(k, k ^ flip) for k in range(size)])


def add_low(left, right):
    return (left.astype(f32) + right.astype(f32)).astype(bf16)


def tie(value, *after):
    return lax.optimization_barrier((value,) + after)[0]


def shard_swap(value, flip, size):
    return lax.ppermute(value, SHARD, [(k, k ^ flip) for k in range(size)])


def gather_shards(value, size):
    outer = [value] + [shard_swap(value, 2 * k, size) for k in range(1, size // 2)]
    pieces = []
    for piece in outer:
        pieces += [piece, shard_swap(piece, 1, size)]
    rows, columns = value.shape
    index = jnp.arange(size, dtype=jnp.int32) ^ lax.axis_index(SHARD).astype(jnp.int32)
    return call(
        functools.partial(join_kernel, size),
        (1,),
        index,
        [whole(value.shape)] * size,
        whole((size * rows, columns)),
        sds((size * rows, columns), value.dtype),
        [out_there(piece) for piece in pieces],
        us=3,
    ), outer[1]


def scatter_outer(kept, given, size):
    count = size // 2
    me = (lax.axis_index(SHARD) // 2).astype(jnp.int32).reshape(1)
    shape = (kept.shape[0] // count, kept.shape[1])
    own, *others = call(
        sum_kernel,
        (1,),
        me,
        [whole(kept.shape)] * 2,
        [whole(shape)] * count,
        [sds(shape, bf16)] * count,
        [kept, given],
        us=2,
    )
    return [own] + [shard_swap(other, 2 * k + 2, size) for k, other in enumerate(others)]


def adamw(param, moments, grad, decay):
    scaled = grad / loss_scale
    first = first_decay * moments[0] + (1.0 - first_decay) * scaled
    second = second_decay * moments[1] + (1.0 - second_decay) * scaled * scaled
    corrected = (
        first
        / (1.0 - first_decay**step_count)
        / (jnp.sqrt(second / (1.0 - second_decay**step_count)) + adam_eps)
    )
    return (param - rate * (corrected + decay * param), jnp.stack([first, second]))


def on_device(
    n_shard,
    n_tensor,
    tokens,
    cotangent,
    input_weight,
    input_moments,
    input_bias,
    input_bias_moments,
    output_weight,
    output_moments,
    expand_weight,
    expand_moments,
    expand_bias,
    expand_bias_moments,
    shrink_weight,
    shrink_moments,
    vectors,
    vector_moments,
):
    rows, d = tokens.shape
    images = rows // SEQ
    per = images // n_tensor
    part = d // n_shard
    width = input_weight.shape[2]
    hidden = expand_weight.shape[1]
    me = lax.axis_index(TENSOR).astype(jnp.int32)
    index = jnp.arange(n_tensor, dtype=jnp.int32) ^ me
    near, far, own = index[:2], index[2:], index[:1]

    n_small = vectors.shape[0] + 1 + input_bias.shape[0]
    pack_one = pack(own, input_weight, output_weight, vectors, expand_bias, input_bias)
    pack_two = jnp.concatenate([expand_weight, shrink_weight.T], axis=1).astype(bf16)
    w_one, first = gather_shards(pack_one, n_shard)
    w_two = lax.all_gather(tie(pack_two, first), SHARD, axis=0, tiled=True)
    small = w_one[:, 4 * width :].reshape(n_shard, part, LANES)[:, :n_small].astype(f32)
    vec = jnp.pad(small[:, :6, :part].transpose(1, 0, 2).reshape(6, d), ((0, 2), (0, 0)))
    full_expand_bias = small[:, 6, :part].reshape(1, hidden)
    full_bias = small[:, 7:9, : width // n_shard].transpose(1, 0, 2).reshape(2, width)

    tok, cot = [padded(own, values, n_tensor) for values in (tokens, cotangent)]
    far = tie(far, cot)
    q_rows = per * PAD
    block = (q_rows, d)

    buffers, (p2, p3) = attn_fwd(far, tok, w_one, vec, full_bias, ())
    sum2 = add_low(p2, swap(p3, 1, n_tensor))
    cross = swap(sum2, 2, n_tensor)
    (inputs_all, qkv_all, ctx_all), (p0, p1) = attn_fwd(tie(near, sum2), tok, w_one, vec, full_bias, buffers)
    sum0 = add_low(p0, swap(p1, 1, n_tensor))
    attended, normed = rowwise(
        mid_kernel, own, [tok, sum0, cross, vec], "qrrw", [far_sds(block, f32), sds(block, bf16)]
    )

    def gather_rows(value):
        return (value, swap(value, 1, n_tensor)), swap(value, 2, n_tensor)

    def gather_far(over, *after):
        over = tie(over, *after)
        return over, swap(over, 1, n_tensor)

    near_x, over_x = gather_rows(normed)
    buffers, bias_near, shrink_near, mid_near = ffn(near, near_x, cot, w_two, full_expand_bias, ())
    far_x = gather_far(over_x, mid_near[0])
    ffn_all, bias_far, shrink_far, mid_far = ffn(far, far_x, cot, w_two, full_expand_bias, buffers)
    x_all, hid_all, pre_all = ffn_all

    def scatter_rows(near_parts, far_parts):
        over = add_low(far_parts[0], swap(far_parts[1], 1, n_tensor))
        return add_low(near_parts[0], swap(near_parts[1], 1, n_tensor)), over

    mid_mine, mid_over = scatter_rows(mid_near, mid_far)
    mid_theirs = swap(mid_over, 2, n_tensor)
    grads_two = weight_grads(tie(own, mid_over), x_all, pre_all, cot, hid_all)
    share_two = lax.psum_scatter(grads_two, SHARD, scatter_dimension=0, tiled=True)
    mid_theirs = tie(mid_theirs, grads_two)
    mid, mid_low, vec_mid = rowwise(
        mid_back_kernel,
        own,
        [attended, cot, mid_mine, mid_theirs, vec],
        "Rqrrw",
        [far_sds(block, f32), sds(block, bf16), sds((8, d), f32)],
    )

    near_m, over_m = gather_rows(mid_low)
    buffers, sums_near, vec_near, part_near = attn_bwd(near, near_m, tok, qkv_all, w_one, ())
    far_m = gather_far(over_m, part_near[0])
    shrink_mine, shrink_over = scatter_rows(shrink_near, shrink_far)
    shrink_theirs = swap(tie(shrink_over, part_near[0]), 2, n_tensor)
    (mid_all, grad_all), sums_far, vec_far, part_far = attn_bwd(far, far_m, tok, qkv_all, w_one, buffers)

    mine, over = scatter_rows(part_near, part_far)
    theirs = swap(over, 2, n_tensor)

    vec_grads = jnp.concatenate([vec_near + vec_far, vec_mid[:4], (bias_near + bias_far).reshape(1, d)])
    vec_grads = vec_grads.reshape(7, n_shard, part).transpose(1, 0, 2)
    vec_grads = jnp.pad(vec_grads, ((0, 0), (0, 0), (0, LANES - part)))
    sums = sums_near + sums_far
    bias_grads = jnp.stack([sums[:width], sums[2 * width :]]).reshape(2, n_shard, -1).transpose(1, 0, 2)
    bias_grads = jnp.pad(bias_grads, ((0, 0), (0, 0), (0, LANES - bias_grads.shape[2])))
    tail = jnp.concatenate([vec_grads, bias_grads], axis=1)
    tail = jnp.pad(tail, ((0, 0), (0, part - n_small), (0, 0))).reshape(d, LANES).astype(bf16)
    grads_one = weight_grads(
        tie(lax.axis_index(SHARD).astype(jnp.int32).reshape(1) % 2, over),
        inputs_all,
        grad_all,
        mid_all,
        ctx_all,
        tail,
        part,
        2 * width,
    )
    halves = [(kept, shard_swap(given, 1, n_shard)) for kept, given in (grads_one[:2], grads_one[2:])]

    theirs = tie(theirs, grads_one[0])
    (token_low,) = rowwise(token_back_kernel, own, [tok, mid, mine, theirs, vec], "qRrrw", [sds(block, bf16)])
    (kept_one, given_one), (kept_two, given_two) = halves
    halves = [scatter_outer(kept_one, tie(given_one, token_low), n_shard), scatter_outer(kept_two, given_two, n_shard)]
    result = attended + (shrink_mine.astype(f32) + shrink_theirs.astype(f32)) + vec[5]
    near_o, over_o = gather_rows(tie(result.astype(bf16), theirs))
    near_t, over_t = gather_rows(token_low)

    share_two = tie(share_two, halves[1][0])
    share_expand, new_expand, mom_expand, share_shrink, new_shrink, mom_shrink = adam_hidden(
        own, share_two, expand_weight, expand_moments, shrink_weight, shrink_moments
    )
    token_gradient = spread(index, near_t + gather_far(over_t, share_expand), f32)
    block_output = spread(index, near_o + gather_far(over_o, token_gradient), bf16)
    first, second = [[tie(half[0], block_output)] + half[1:] for half in halves]
    share_input, new_input, mom_input, share_output, new_output, mom_output, small = adam_attention(
        own, first, second, input_weight, input_moments, output_weight, output_moments
    )
    own_vectors = small[:6, :part]
    share_vectors = functools.reduce(
        jnp.add, [own_vectors] + [swap(own_vectors, k, n_tensor) for k in range(1, n_tensor)]
    )
    share_expand_bias = small[6, :part]
    share_bias = small[7:9, : width // n_shard]

    new_bias, mom_bias = adamw(input_bias, input_bias_moments, share_bias, 0.0)
    new_expand_bias, mom_expand_bias = adamw(
        expand_bias, expand_bias_moments, share_expand_bias, 0.0
    )
    new_vectors, mom_vectors = adamw(vectors, vector_moments, share_vectors, 0.0)
    return (
        block_output,
        token_gradient,
        share_input,
        share_bias,
        share_output,
        share_expand,
        share_expand_bias,
        share_shrink,
        share_vectors,
        new_input,
        new_bias,
        new_output,
        new_expand,
        new_expand_bias,
        new_shrink,
        new_vectors,
        mom_input,
        mom_bias,
        mom_output,
        mom_expand,
        mom_expand_bias,
        mom_shrink,
        mom_vectors,
    )


def solution(mesh):
    def body(*args):
        return on_device(mesh.shape[SHARD], mesh.shape[TENSOR], *args)

    return jax.shard_map(
        body,
        mesh=mesh,
        in_specs=(
            P(SHARD, None),
            P(SHARD, None),
            P(None, SHARD, TENSOR),
            P(None, None, SHARD, TENSOR),
            P(None, (TENSOR, SHARD)),
            P(None, None, (TENSOR, SHARD)),
            P(TENSOR, SHARD),
            P(None, TENSOR, SHARD),
            P(SHARD, TENSOR),
            P(None, SHARD, TENSOR),
            P((TENSOR, SHARD)),
            P(None, (TENSOR, SHARD)),
            P(TENSOR, SHARD),
            P(None, TENSOR, SHARD),
            P(None, SHARD),
            P(None, None, SHARD),
        ),
        out_specs=(
            P(SHARD, None),
            P(SHARD, None),
            P(None, SHARD, TENSOR),
            P(None, (TENSOR, SHARD)),
            P(TENSOR, SHARD),
            P(SHARD, TENSOR),
            P((TENSOR, SHARD)),
            P(TENSOR, SHARD),
            P(None, SHARD),
            P(None, SHARD, TENSOR),
            P(None, (TENSOR, SHARD)),
            P(TENSOR, SHARD),
            P(SHARD, TENSOR),
            P((TENSOR, SHARD)),
            P(TENSOR, SHARD),
            P(None, SHARD),
            P(None, None, SHARD, TENSOR),
            P(None, None, (TENSOR, SHARD)),
            P(None, TENSOR, SHARD),
            P(None, SHARD, TENSOR),
            P(None, (TENSOR, SHARD)),
            P(None, TENSOR, SHARD),
            P(None, None, SHARD),
        ),
        check_vma=False,
    )
```

```python
import functools

import jax
import jax.numpy as jnp
from jax import lax
from jax.experimental import pallas as pl
from jax.experimental.pallas import tpu as pltpu
from jax.sharding import PartitionSpec as P


HEAD = 64
SEQ = 197
PAD = 208
LANES = 128
SHARD, TENSOR = "shard", "tensor"

norm_eps = 1e-06
rate = 0.003
first_decay = 0.9
second_decay = 0.95
weight_decay = 0.05
step_count = 2.0
adam_eps = 1e-08
loss_scale = 128.0


bf16 = jnp.bfloat16
f32 = jnp.float32
NT = (((1,), (1,)), ((), ()))
TN = (((0,), (0,)), ((), ()))
PARAMS = pltpu.CompilerParams(vmem_limit_bytes=40 * 1024 * 1024)


def dot(left, right):
    return jnp.dot(left, right, preferred_element_type=f32)


def dot_nt(left, right):
    return lax.dot_general(left, right, NT, preferred_element_type=f32)


def dot_tn(left, right):
    return lax.dot_general(left, right, TN, preferred_element_type=f32)


def whole(shape):
    return pl.BlockSpec(shape, lambda i, idx: (0,) * len(shape))


def picked(shape):
    return pl.BlockSpec((1,) + shape, lambda i, idx: (idx[i],) + (0,) * len(shape))


def store_one(refs, i, value):
    for j, ref in enumerate(refs):

        @pl.when(i == j)
        def _():
            ref[...] = value


def load_one(refs, i, scratch):
    for j, ref in enumerate(refs):

        @pl.when(i == j)
        def _():
            scratch[...] = ref[...]

    return scratch[...]


def norm_stats(values):
    centred = values - jnp.mean(values, axis=-1, keepdims=True)
    spread = jnp.mean(centred * centred, axis=-1, keepdims=True)
    inverse = lax.rsqrt(spread + norm_eps)
    return centred * inverse, inverse


def norm_back(unit, inverse, grad, gain):
    scaled = grad * gain
    mean_one = jnp.mean(scaled, axis=-1, keepdims=True)
    mean_two = jnp.mean(scaled * unit, axis=-1, keepdims=True)
    return inverse * (scaled - mean_one - unit * mean_two)


def attn_fwd_kernel(width, shared, idx, tok, w, vec, bias, *rest):
    rest = rest[shared:]
    inputs_out, qkv_out, ctx_out = rest[:3]
    parts = rest[3:]
    i = pl.program_id(0)
    unit, _ = norm_stats(tok[0].astype(f32))
    inputs = (unit * vec[0:1, :] + vec[1:2, :]).astype(bf16)
    inputs_out[0] = inputs
    project = dot(inputs, w[:, : 3 * width])
    query = (project[:, :width] + bias[0:1, :]).astype(bf16)
    keys = project[:, width : 2 * width].astype(bf16)
    values = (project[:, 2 * width :] + bias[1:2, :]).astype(bf16)
    qkv_out[0, :, :width] = query
    qkv_out[0, :, width : 2 * width] = keys
    qkv_out[0, :, 2 * width :] = values
    scale = bf16(HEAD ** (-0.5))
    lane = lax.broadcasted_iota(jnp.int32, (1, LANES), 1)
    live = lax.broadcasted_iota(jnp.int32, (1, PAD), 1) < SEQ

    def one_image(image, _):
        rows = pl.ds(pl.multiple_of(image * PAD, PAD), PAD)
        for pair in range(width // LANES):
            at = [slice(c * width + pair * LANES, c * width + (pair + 1) * LANES) for c in range(3)]
            q2, k2, v2 = qkv_out[0, rows, at[0]] * scale, qkv_out[0, rows, at[1]], qkv_out[0, rows, at[2]]
            outs = []
            for half in range(LANES // HEAD):
                mine = (lane // HEAD) == half
                scores = dot_nt(jnp.where(mine, q2, bf16(0)), k2)
                scores = jnp.where(live, scores, -1e30)
                raised = jnp.exp(scores - jnp.max(scores, axis=-1, keepdims=True))
                total = jnp.sum(raised, axis=-1, keepdims=True)
                outs.append(dot((raised * (1.0 / total)).astype(bf16), v2))
            ctx_out[0, rows, at[0]] = jnp.where(lane < HEAD, outs[0], outs[1]).astype(bf16)
        return 0

    lax.fori_loop(0, tok.shape[1] // PAD, one_image, 0)
    store_one(parts, i, dot_nt(ctx_out[0], w[:, 3 * width : 4 * width]).astype(bf16))


def ffn_kernel(nq, shared, idx, *refs):
    pieces, (cot, w, bias) = refs[:nq], refs[nq : nq + 3]
    refs = refs[nq + 3 + shared :]
    x_out, hid_out, pre_out, bias_out = refs[:4]
    shrink_parts, mid_parts, scratch = refs[4 : 4 + nq], refs[4 + nq : 4 + 2 * nq], refs[-1]
    i = pl.program_id(0)
    width = bias.shape[1]
    x = load_one(pieces, i, scratch)
    x_out[0] = x
    back = cot[0]

    @pl.when(i == 0)
    def _():
        bias_out[...] = jnp.zeros_like(bias_out)

    step = 512

    def some_columns(k, _):
        start = pl.multiple_of(k * step, step)
        cols, second = pl.ds(start, step), pl.ds(width + start, step)
        pre = dot(x, w[:, cols]) + bias[0:1, cols]
        grad = dot(back, w[:, second])
        share = 0.5 + 0.5 * lax.erf(pre * (0.5**0.5))
        slope = share + pre * (jnp.exp(-0.5 * pre * pre) * 0.3989422804014327)
        hid_out[0, :, cols] = (pre * share).astype(bf16)
        pre_grad = (slope * grad).astype(bf16)
        pre_out[0, :, cols] = pre_grad
        bias_out[0:1, cols] += jnp.sum(pre_grad.astype(f32), axis=0, keepdims=True)
        return 0

    lax.fori_loop(0, width // step, some_columns, 0)

    def some_outputs(k, _):
        at = pl.ds(pl.multiple_of(k * step, step), step)
        for ref, value, start in ((shrink_parts, hid_out, width), (mid_parts, pre_out, 0)):
            part = dot_nt(value[0], w[at, start : start + width]).astype(bf16)
            for j in range(nq):

                @pl.when(i == j)
                def _():
                    ref[j][:, at] = part

        return 0

    lax.fori_loop(0, x.shape[1] // step, some_outputs, 0)


def attn_bwd_kernel(nq, width, shared, idx, *refs):
    pieces, (tok, qkv, w) = refs[:nq], refs[nq : nq + 3]
    refs = refs[nq + 3 + shared :]
    mid_out, grad_out, sums_out, vec_out = refs[:4]
    parts, scratch, ctx_grads = refs[4 : 4 + nq], refs[-2], refs[-1]
    i = pl.program_id(0)
    mid = load_one(pieces, i, scratch)
    mid_out[0] = mid
    ctx_grad = dot(mid, w[:, 3 * width : 4 * width]).astype(bf16)
    scale = bf16(HEAD ** (-0.5))
    lane = lax.broadcasted_iota(jnp.int32, (1, LANES), 1)
    live = lax.broadcasted_iota(jnp.int32, (PAD, 1), 0) < SEQ

    ctx_grads[...] = ctx_grad

    pairs = width // LANES

    def one_pair(step, _):
        rows = pl.ds(pl.multiple_of(step // pairs * PAD, PAD), PAD)
        start = step % pairs * LANES
        at = [pl.ds(pl.multiple_of(c * width + start, LANES), LANES) for c in range(3)]
        q2, k2, v2 = qkv[0, rows, at[0]] * scale, qkv[0, rows, at[1]], qkv[0, rows, at[2]]
        c2 = ctx_grads[rows, at[0]]
        outs = []
        for half in range(LANES // HEAD):
            mine = (lane // HEAD) == half
            scores = dot_nt(k2, jnp.where(mine, q2, bf16(0)))
            scores = jnp.where(live, scores, -1e30)
            raised = jnp.exp(scores - jnp.max(scores, axis=0, keepdims=True))
            prob = raised * (1.0 / jnp.sum(raised, axis=0, keepdims=True))
            prob_grad = dot_nt(v2, jnp.where(mine, c2, bf16(0)))
            row_dot = jnp.sum(prob_grad * prob, axis=0, keepdims=True)
            score_grad = (prob * (prob_grad - row_dot)).astype(bf16)
            outs.append(
                (
                    dot_tn(score_grad, k2) * HEAD ** (-0.5),
                    dot(score_grad, q2),
                    dot(prob.astype(bf16), c2),
                )
            )
        for c in range(3):
            grad_out[0, rows, at[c]] = jnp.where(lane < HEAD, outs[0][c], outs[1][c]).astype(bf16)
        return 0

    lax.fori_loop(0, tok.shape[1] // PAD * pairs, one_pair, 0)
    grads = grad_out[0]
    part = dot_nt(grads, w[:, : 3 * width])
    store_one(parts, i, part.astype(bf16))
    unit, _ = norm_stats(tok[0].astype(f32))

    @pl.when(i == 0)
    def _():
        sums_out[...] = jnp.zeros_like(sums_out)
        vec_out[...] = jnp.zeros_like(vec_out)

    sums_out[0:1, :] += jnp.sum(grads.astype(f32), axis=0, keepdims=True)
    vec_out[0:1, :] += jnp.sum(part * unit, axis=0, keepdims=True)
    vec_out[1:2, :] += jnp.sum(part, axis=0, keepdims=True)


def mid_kernel(idx, tok, mine, theirs, vec, attended_out, normed_out):
    attended = tok[0].astype(f32) + (mine[...].astype(f32) + theirs[...].astype(f32)) + vec[2:3, :]
    attended_out[...] = attended
    unit, _ = norm_stats(attended)
    normed_out[...] = (unit * vec[3:4, :] + vec[4:5, :]).astype(bf16)


def mid_back_kernel(idx, attended, cot, mine, theirs, vec, mid_out, low_out, sums_out):
    grad = mine[...].astype(f32) + theirs[...].astype(f32)
    unit, inverse = norm_stats(attended[...])
    back = cot[0].astype(f32)
    mid = back + norm_back(unit, inverse, grad, vec[3:4, :])
    mid_out[...] = mid
    low_out[...] = mid.astype(bf16)

    @pl.when(pl.program_id(0) == 0)
    def _():
        sums_out[...] = jnp.zeros_like(sums_out)

    sums_out[0:1, :] += jnp.sum(mid, axis=0, keepdims=True)
    sums_out[1:2, :] += jnp.sum(grad * unit, axis=0, keepdims=True)
    sums_out[2:3, :] += jnp.sum(grad, axis=0, keepdims=True)
    sums_out[3:4, :] += jnp.sum(back, axis=0, keepdims=True)


def token_back_kernel(idx, tok, mid, mine, theirs, vec, out):
    grad = mine[...].astype(f32) + theirs[...].astype(f32)
    unit, inverse = norm_stats(tok[0].astype(f32))
    out[...] = (mid[...] + norm_back(unit, inverse, grad, vec[0:1, :])).astype(bf16)


def spread_kernel(nq, idx, *refs):
    pieces, out, flat = refs[:nq], refs[nq], refs[nq + 1]

    def some_columns(k, _):
        cols = pl.ds(pl.multiple_of(k * LANES, LANES), LANES)
        for j, piece in enumerate(pieces):
            images = piece.shape[0] // PAD
            for image in range(images):
                value = piece[image * PAD : (image + 1) * PAD, cols].astype(f32)
                flat[pl.ds((idx[j] * images + image) * SEQ, SEQ), :] = value[:SEQ]
        out[:, cols] = flat[...].astype(out.dtype)
        return 0

    lax.fori_loop(0, out.shape[1] // LANES, some_columns, 0)


def join_kernel(size, idx, *refs):
    pieces, out = refs[:size], refs[size]
    rows = pieces[0].shape[0]
    for j, piece in enumerate(pieces):
        out[pl.ds(pl.multiple_of(idx[j] * rows, rows), rows), :] = piece[...]


def weight_grad_kernel(idx, left_one, right_one, left_two, right_two, out):
    first = right_one.shape[1]
    out[:, :first] = dot_tn(left_one[...], right_one[...]).astype(bf16)
    out[:, first:] = dot_tn(left_two[...], right_two[...]).astype(bf16)


def split_grad_kernel(part, cut, idx, left_one, right_one, left_two, right_two, tail, *outs):
    i = pl.program_id(0)
    value = jnp.concatenate(
        [
            dot_tn(left_one[...], right_one[...]).astype(bf16),
            dot_tn(left_two[...], right_two[...]).astype(bf16),
            tail[...],
        ],
        axis=1,
    )
    blocks = value.shape[0] // part
    for block in range(blocks):
        at = pl.ds(pl.multiple_of((i * (blocks // 2) + block // 2) * part, part), part)
        rows = value[block * part : (block + 1) * part]
        for given in range(2):

            @pl.when((idx[0] == block % 2) != bool(given))
            def _():
                outs[given][at, :] = rows[:, :cut]
                outs[2 + given][at, :] = rows[:, cut:]


def adam_values(param, first, second, grad, decay):
    scaled = grad / loss_scale
    first = first_decay * first + (1.0 - first_decay) * scaled
    second = second_decay * second + (1.0 - second_decay) * scaled * scaled
    corrected = (
        first
        / (1.0 - first_decay**step_count)
        / (jnp.sqrt(second / (1.0 - second_decay**step_count)) + adam_eps)
    )
    return param - rate * (corrected + decay * param), first, second


def adam_store(value, p, m, share_out, new_out, mom_out):
    share_out[...] = value
    new_out[...], mom_out[0], mom_out[1] = adam_values(p[...], m[0], m[1], value, weight_decay)


def adam_hidden_kernel(idx, grad, turned_grad, param, moments, turned, turned_moments, *outs):
    adam_store(grad[...].astype(f32), param, moments, *outs[:3])
    adam_store(turned_grad[...].astype(f32).T, turned, turned_moments, *outs[3:])


def adam_attention_kernel(n, idx, *refs):
    first, second, (param, moments, turned, turned_moments), outs = refs[:n], refs[n : 2 * n], refs[2 * n : 2 * n + 4], refs[2 * n + 4 :]
    one = functools.reduce(jnp.add, [ref[...].astype(f32) for ref in first])
    two = functools.reduce(jnp.add, [ref[...].astype(f32) for ref in second])
    width = param.shape[2]
    for c, value in enumerate((one[:, :width], one[:, width:], two[:, :width])):
        adam_store(value, param.at[c], moments.at[:, c], outs[0].at[c], outs[1].at[c], outs[2].at[:, c])
    adam_store(two[:, width : 2 * width].T, turned, turned_moments, *outs[3:6])


def sum_kernel(idx, kept, given, *outs):
    rows = outs[0].shape[0]
    for k, out in enumerate(outs):
        at = pl.ds(pl.multiple_of((idx[0] ^ k) * rows, rows), rows)
        out[...] = (kept[at, :].astype(f32) + given[at, :].astype(f32)).astype(bf16)


def pad_kernel(idx, values, out, flat):
    rows = values.shape[0]
    live = lax.broadcasted_iota(jnp.int32, (PAD, 1), 0) < SEQ
    per = out.shape[1] // PAD

    def some_columns(k, _):
        cols = pl.ds(pl.multiple_of(k * LANES, LANES), LANES)
        flat[:rows, :] = values[:, cols].astype(f32)
        for image in range(rows // SEQ):
            value = jnp.where(live, flat[image * SEQ : image * SEQ + PAD, :], 0.0)
            at = slice(image % per * PAD, (image % per + 1) * PAD)
            out[image // per, at, cols] = value.astype(bf16)
        return 0

    lax.fori_loop(0, values.shape[1] // LANES, some_columns, 0)


def pack_kernel(idx, inner, outer, vectors, hidden_bias, bias, out, small):
    part, width = inner.shape[1:]
    for c in range(3):
        out[:, c * width : (c + 1) * width] = inner[c].astype(bf16)
    out[:, 3 * width : 4 * width] = outer[...].T.astype(bf16)
    small[...] = jnp.zeros_like(small)
    small[0:6, :part] = vectors[...]
    small[6:7, :part] = hidden_bias[...]
    small[7:9, : bias.shape[1]] = bias[...]
    out[:, 4 * width :] = small[...].astype(bf16)


def call(kernel, grid, idx, in_specs, out_specs, out_shapes, args, aliases=None, scratch=(), us=5):
    return pl.pallas_call(
        kernel,
        grid_spec=pltpu.PrefetchScalarGridSpec(
            num_scalar_prefetch=1,
            grid=grid,
            in_specs=in_specs,
            out_specs=out_specs,
            scratch_shapes=list(scratch),
        ),
        out_shape=out_shapes,
        input_output_aliases=aliases or {},
        compiler_params=PARAMS,
        cost_estimate=pl.CostEstimate(flops=us * 10**9, bytes_accessed=us * 3 * 10**6, transcendentals=0),
    )(idx, *args)


def sds(shape, dtype):
    return jax.ShapeDtypeStruct(shape, dtype)


def far_sds(shape, dtype):
    return pltpu.HBM(shape, dtype)


def out_there(value):
    return pltpu.with_memory_space_constraint(value, pltpu.HBM)


def shared_args(buffers, n_args):
    specs = [pl.BlockSpec(memory_space=pl.ANY)] * len(buffers)
    aliases = {1 + n_args + j: j for j in range(len(buffers))}
    return specs, list(buffers), aliases


def attn_fwd(idx, tok, w, vec, bias, buffers):
    nq, (quarters, rows, d), width = idx.shape[0], tok.shape, bias.shape[1]
    specs, extra, aliases = shared_args(buffers, 4)
    out = call(
        functools.partial(attn_fwd_kernel, width, len(buffers)),
        (nq,),
        idx,
        [picked((rows, d)), whole(w.shape), whole(vec.shape), whole(bias.shape)] + specs,
        [picked((rows, d)), picked((rows, 3 * width)), picked((rows, width))] + [whole((rows, d))] * nq,
        [far_sds((quarters, rows, n), bf16) for n in (d, 3 * width, width)] + [sds((rows, d), bf16)] * nq,
        [out_there(tok), w, vec, bias] + extra,
        aliases,
        us=12,
    )
    return out[:3], out[3:]


def ffn(idx, pieces, cot, w, bias, buffers):
    nq, (quarters, rows, d), width = idx.shape[0], cot.shape, bias.shape[1]
    specs, extra, aliases = shared_args(buffers, nq + 3)
    out = call(
        functools.partial(ffn_kernel, nq, len(buffers)),
        (nq,),
        idx,
        [whole((rows, d))] * nq + [picked((rows, d)), whole(w.shape), whole(bias.shape)] + specs,
        [picked((rows, d)), picked((rows, width)), picked((rows, width)), whole((8, width))]
        + [whole((rows, d))] * (2 * nq),
        [far_sds((quarters, rows, n), bf16) for n in (d, width, width)]
        + [sds((8, width), f32)]
        + [sds((rows, d), bf16)] * (2 * nq),
        list(pieces) + [out_there(cot), w, bias] + extra,
        aliases,
        [pltpu.VMEM((rows, d), bf16)],
        us=16,
    )
    return out[:3], out[3][0], out[4 : 4 + nq], out[4 + nq :]


def attn_bwd(idx, pieces, tok, qkv, w, buffers):
    nq, (quarters, rows, d), width = idx.shape[0], tok.shape, qkv.shape[2] // 3
    specs, extra, aliases = shared_args(buffers, nq + 3)
    out = call(
        functools.partial(attn_bwd_kernel, nq, width, len(buffers)),
        (nq,),
        idx,
        [whole((rows, d))] * nq + [picked((rows, d)), picked((rows, 3 * width)), whole(w.shape)] + specs,
        [picked((rows, d)), picked((rows, 3 * width)), whole((8, 3 * width)), whole((8, d))]
        + [whole((rows, d))] * nq,
        [far_sds((quarters, rows, d), bf16), far_sds((quarters, rows, 3 * width), bf16)]
        + [sds((8, 3 * width), f32), sds((8, d), f32)]
        + [sds((rows, d), bf16)] * nq,
        list(pieces) + [out_there(tok), out_there(qkv), w] + extra,
        aliases,
        [pltpu.VMEM((rows, d), bf16), pltpu.VMEM((rows, width), bf16)],
        us=16,
    )
    return out[:2], out[2][0], out[3][:2], out[4:]


def rowwise(kernel, idx, args, kinds, outs):
    rows, d = outs[0].shape
    steps = rows // PAD
    specs = {
        "q": lambda v: pl.BlockSpec((1, PAD, d), lambda i, idx: (idx[0], i, 0)),
        "r": lambda v: pl.BlockSpec((PAD, d), lambda i, idx: (i, 0)),
        "w": lambda v: whole(v.shape),
    }
    return call(
        kernel,
        (steps,),
        idx,
        [specs[kind.lower()](v) for kind, v in zip(kinds, args)],
        [specs["w" if o.shape[0] == 8 else "r"](o) for o in outs],
        outs,
        [out_there(v) if kind in "qR" else v for kind, v in zip(kinds, args)],
        us=3,
    )


def weight_grads(idx, left_one, right_one, left_two, right_two, tail=None, part=None, cut=None):
    d = left_one.shape[2]
    flat = [out_there(v.reshape(-1, v.shape[2])) for v in (left_one, right_one, left_two, right_two)]
    first, second = flat[1].shape[1], flat[3].shape[1]
    step = 256
    n = flat[0].shape[0]
    column = pl.BlockSpec((n, step), lambda i, idx: (0, i))
    specs = [column, whole((n, first)), column, whole((n, second))]
    if tail is None:
        return call(
            weight_grad_kernel,
            (d // step,),
            idx,
            specs,
            pl.BlockSpec((step, first + second), lambda i, idx: (i, 0)),
            sds((d, first + second), bf16),
            flat,
            us=14,
        )
    shapes = [(d // 2, cut)] * 2 + [(d // 2, first + second + tail.shape[1] - cut)] * 2
    return call(
        functools.partial(split_grad_kernel, part, cut),
        (d // step,),
        idx,
        specs + [pl.BlockSpec((step, tail.shape[1]), lambda i, idx: (i, 0))],
        [whole(shape) for shape in shapes],
        [sds(shape, bf16) for shape in shapes],
        flat + [tail],
        us=10,
    )


def adam_hidden(idx, grads, param, moments, turned, turned_moments):
    part, hidden = param.shape
    step = 256
    count = hidden // step
    wide = pl.BlockSpec((part, step), lambda i, idx: (0, i))
    wide_two = pl.BlockSpec((2, part, step), lambda i, idx: (0, 0, i))
    tall = pl.BlockSpec((step, part), lambda i, idx: (i, 0))
    tall_two = pl.BlockSpec((2, step, part), lambda i, idx: (0, i, 0))
    beside = pl.BlockSpec((part, step), lambda i, idx: (0, i + count))
    outs = [sds(v.shape, f32) for v in (param, param, moments, turned, turned, turned_moments)]
    return call(
        adam_hidden_kernel,
        (count,),
        idx,
        [wide, beside, wide, wide_two, tall, tall_two],
        [wide, wide, wide_two, tall, tall, tall_two],
        outs,
        [out_there(v) for v in (grads, grads, param, moments, turned, turned_moments)],
        us=4,
    )


def adam_attention(idx, first, second, param, moments, turned, turned_moments):
    args = list(first) + list(second) + [out_there(v) for v in (param, moments, turned, turned_moments)]
    outs = [sds(v.shape, f32) for v in (param, param, moments, turned, turned, turned_moments)]
    return call(
        functools.partial(adam_attention_kernel, len(first)),
        (1,),
        idx,
        [whole(v.shape) for v in args],
        [whole(o.shape) for o in outs],
        outs,
        args,
        us=3,
    )


def padded(idx, values, quarters):
    rows, d = values.shape
    images = rows // SEQ
    shape = (quarters, images // quarters * PAD, d)
    step = d // 2
    return call(
        pad_kernel,
        (d // step,),
        idx,
        [pl.BlockSpec((rows, step), lambda i, idx: (0, i))],
        pl.BlockSpec(shape[:2] + (step,), lambda i, idx: (0, 0, i)),
        far_sds(shape, bf16),
        [values],
        scratch=[pltpu.VMEM(((images - 1) * SEQ + PAD + 5, LANES), f32)],
        us=4,
    )


def pack(idx, inner, outer, vectors, hidden_bias, bias):
    part, width = inner.shape[1:]
    args = [out_there(v) for v in (inner, outer, vectors, hidden_bias.reshape(1, -1), bias)]
    shape = (part, 4 * width + LANES)
    return call(
        pack_kernel,
        (1,),
        idx,
        [whole(v.shape) for v in args],
        whole(shape),
        sds(shape, bf16),
        args,
        scratch=[pltpu.VMEM((part, LANES), f32)],
        us=2,
    )


def spread(idx, pieces, dtype):
    rows, d = pieces[0].shape
    total = len(pieces) * rows // PAD * SEQ
    step = d // 2
    return call(
        functools.partial(spread_kernel, len(pieces)),
        (d // step,),
        idx,
        [pl.BlockSpec((rows, step), lambda i, idx: (0, i))] * len(pieces),
        pl.BlockSpec((total, step), lambda i, idx: (0, i)),
        sds((total, d), dtype),
        list(pieces),
        scratch=[pltpu.VMEM((total, LANES), f32)],
        us=4,
    )


def swap(value, flip, size):
    return lax.ppermute(value, TENSOR, [(k, k ^ flip) for k in range(size)])


def add_low(left, right):
    return (left.astype(f32) + right.astype(f32)).astype(bf16)


def tie(value, *after):
    return lax.optimization_barrier((value,) + after)[0]


def shard_swap(value, flip, size):
    return lax.ppermute(value, SHARD, [(k, k ^ flip) for k in range(size)])


def gather_shards(value, size):
    outer = [value] + [shard_swap(value, 2 * k, size) for k in range(1, size // 2)]
    pieces = []
    for piece in outer:
        pieces += [piece, shard_swap(piece, 1, size)]
    rows, columns = value.shape
    index = jnp.arange(size, dtype=jnp.int32) ^ lax.axis_index(SHARD).astype(jnp.int32)
    return call(
        functools.partial(join_kernel, size),
        (1,),
        index,
        [whole(value.shape)] * size,
        whole((size * rows, columns)),
        sds((size * rows, columns), value.dtype),
        [out_there(piece) for piece in pieces],
        us=3,
    ), outer[1]


def scatter_outer(kept, given, size):
    count = size // 2
    me = (lax.axis_index(SHARD) // 2).astype(jnp.int32).reshape(1)
    shape = (kept.shape[0] // count, kept.shape[1])
    own, *others = call(
        sum_kernel,
        (1,),
        me,
        [whole(kept.shape)] * 2,
        [whole(shape)] * count,
        [sds(shape, bf16)] * count,
        [kept, given],
        us=2,
    )
    return [own] + [shard_swap(other, 2 * k + 2, size) for k, other in enumerate(others)]


def adamw(param, moments, grad, decay):
    scaled = grad / loss_scale
    first = first_decay * moments[0] + (1.0 - first_decay) * scaled
    second = second_decay * moments[1] + (1.0 - second_decay) * scaled * scaled
    corrected = (
        first
        / (1.0 - first_decay**step_count)
        / (jnp.sqrt(second / (1.0 - second_decay**step_count)) + adam_eps)
    )
    return (param - rate * (corrected + decay * param), jnp.stack([first, second]))


def on_device(
    n_shard,
    n_tensor,
    tokens,
    cotangent,
    input_weight,
    input_moments,
    input_bias,
    input_bias_moments,
    output_weight,
    output_moments,
    expand_weight,
    expand_moments,
    expand_bias,
    expand_bias_moments,
    shrink_weight,
    shrink_moments,
    vectors,
    vector_moments,
):
    rows, d = tokens.shape
    images = rows // SEQ
    per = images // n_tensor
    part = d // n_shard
    width = input_weight.shape[2]
    hidden = expand_weight.shape[1]
    me = lax.axis_index(TENSOR).astype(jnp.int32)
    index = jnp.arange(n_tensor, dtype=jnp.int32) ^ me
    near, far, own = index[:2], index[2:], index[:1]

    n_small = vectors.shape[0] + 1 + input_bias.shape[0]
    pack_one = pack(own, input_weight, output_weight, vectors, expand_bias, input_bias)
    pack_two = jnp.concatenate([expand_weight, shrink_weight.T], axis=1).astype(bf16)
    w_one, first = gather_shards(pack_one, n_shard)
    w_two = lax.all_gather(tie(pack_two, first), SHARD, axis=0, tiled=True)
    small = w_one[:, 4 * width :].reshape(n_shard, part, LANES)[:, :n_small].astype(f32)
    vec = jnp.pad(small[:, :6, :part].transpose(1, 0, 2).reshape(6, d), ((0, 2), (0, 0)))
    full_expand_bias = small[:, 6, :part].reshape(1, hidden)
    full_bias = small[:, 7:9, : width // n_shard].transpose(1, 0, 2).reshape(2, width)

    tok, cot = [padded(own, values, n_tensor) for values in (tokens, cotangent)]
    far = tie(far, cot)
    q_rows = per * PAD
    block = (q_rows, d)

    buffers, (p2, p3) = attn_fwd(far, tok, w_one, vec, full_bias, ())
    sum2 = add_low(p2, swap(p3, 1, n_tensor))
    cross = swap(sum2, 2, n_tensor)
    (inputs_all, qkv_all, ctx_all), (p0, p1) = attn_fwd(tie(near, sum2), tok, w_one, vec, full_bias, buffers)
    sum0 = add_low(p0, swap(p1, 1, n_tensor))
    attended, normed = rowwise(
        mid_kernel, own, [tok, sum0, cross, vec], "qrrw", [far_sds(block, f32), sds(block, bf16)]
    )

    def gather_rows(value):
        return (value, swap(value, 1, n_tensor)), swap(value, 2, n_tensor)

    def gather_far(over, *after):
        over = tie(over, *after)
        return over, swap(over, 1, n_tensor)

    near_x, over_x = gather_rows(normed)
    buffers, bias_near, shrink_near, mid_near = ffn(near, near_x, cot, w_two, full_expand_bias, ())
    far_x = gather_far(over_x, mid_near[0])
    ffn_all, bias_far, shrink_far, mid_far = ffn(far, far_x, cot, w_two, full_expand_bias, buffers)
    x_all, hid_all, pre_all = ffn_all

    def scatter_rows(near_parts, far_parts):
        over = add_low(far_parts[0], swap(far_parts[1], 1, n_tensor))
        return add_low(near_parts[0], swap(near_parts[1], 1, n_tensor)), over

    mid_mine, mid_over = scatter_rows(mid_near, mid_far)
    mid_theirs = swap(mid_over, 2, n_tensor)
    grads_two = weight_grads(tie(own, mid_over), x_all, pre_all, cot, hid_all)
    share_two = lax.psum_scatter(grads_two, SHARD, scatter_dimension=0, tiled=True)
    mid_theirs = tie(mid_theirs, grads_two)
    mid, mid_low, vec_mid = rowwise(
        mid_back_kernel,
        own,
        [attended, cot, mid_mine, mid_theirs, vec],
        "Rqrrw",
        [far_sds(block, f32), sds(block, bf16), sds((8, d), f32)],
    )

    near_m, over_m = gather_rows(mid_low)
    buffers, sums_near, vec_near, part_near = attn_bwd(near, near_m, tok, qkv_all, w_one, ())
    far_m = gather_far(over_m, part_near[0])
    shrink_mine, shrink_over = scatter_rows(shrink_near, shrink_far)
    shrink_theirs = swap(tie(shrink_over, part_near[0]), 2, n_tensor)
    (mid_all, grad_all), sums_far, vec_far, part_far = attn_bwd(far, far_m, tok, qkv_all, w_one, buffers)

    mine, over = scatter_rows(part_near, part_far)
    theirs = swap(over, 2, n_tensor)

    vec_grads = jnp.concatenate([vec_near + vec_far, vec_mid[:4], (bias_near + bias_far).reshape(1, d)])
    vec_grads = vec_grads.reshape(7, n_shard, part).transpose(1, 0, 2)
    vec_grads = jnp.pad(vec_grads, ((0, 0), (0, 0), (0, LANES - part)))
    sums = sums_near + sums_far
    bias_grads = jnp.stack([sums[:width], sums[2 * width :]]).reshape(2, n_shard, -1).transpose(1, 0, 2)
    bias_grads = jnp.pad(bias_grads, ((0, 0), (0, 0), (0, LANES - bias_grads.shape[2])))
    tail = jnp.concatenate([vec_grads, bias_grads], axis=1)
    tail = jnp.pad(tail, ((0, 0), (0, part - n_small), (0, 0))).reshape(d, LANES).astype(bf16)
    grads_one = weight_grads(
        tie(lax.axis_index(SHARD).astype(jnp.int32).reshape(1) % 2, over),
        inputs_all,
        grad_all,
        mid_all,
        ctx_all,
        tail,
        part,
        2 * width,
    )
    halves = [(kept, shard_swap(given, 1, n_shard)) for (kept, given) in (grads_one[:2], grads_one[2:])]

    theirs = tie(theirs, grads_one[0])
    (token_low,) = rowwise(token_back_kernel, own, [tok, mid, mine, theirs, vec], "qRrrw", [sds(block, bf16)])
    (kept_one, given_one), (kept_two, given_two) = halves
    halves = [scatter_outer(kept_one, tie(given_one, token_low), n_shard), scatter_outer(kept_two, given_two, n_shard)]
    result = attended + (shrink_mine.astype(f32) + shrink_theirs.astype(f32)) + vec[5]
    near_o, over_o = gather_rows(tie(result.astype(bf16), theirs))
    near_t, over_t = gather_rows(token_low)

    share_two = tie(share_two, halves[1][0])
    share_expand, new_expand, mom_expand, share_shrink, new_shrink, mom_shrink = adam_hidden(
        own, share_two, expand_weight, expand_moments, shrink_weight, shrink_moments
    )
    token_gradient = spread(index, near_t + gather_far(over_t, share_expand), f32)
    small = functools.reduce(jnp.add, [piece[:n_small, 2 * width :].astype(f32) for piece in [tie(halves[1][0], token_gradient)] + halves[1][1:]])
    own_vectors = small[:6, :part]
    swapped = [swap(own_vectors, k, n_tensor) for k in range(1, n_tensor)]
    block_output = spread(index, near_o + gather_far(over_o, token_gradient), bf16)
    first, second = [[tie(half[0], block_output)] + half[1:] for half in halves]
    share_input, new_input, mom_input, share_output, new_output, mom_output = adam_attention(
        own, first, second, input_weight, input_moments, output_weight, output_moments
    )
    share_vectors = functools.reduce(jnp.add, [own_vectors] + swapped)
    share_expand_bias = small[6, :part]
    share_bias = small[7:9, : width // n_shard]

    new_bias, mom_bias = adamw(input_bias, input_bias_moments, share_bias, 0.0)
    new_expand_bias, mom_expand_bias = adamw(
        expand_bias, expand_bias_moments, share_expand_bias, 0.0
    )
    new_vectors, mom_vectors = adamw(vectors, vector_moments, share_vectors, 0.0)
    return (
        block_output,
        token_gradient,
        share_input,
        share_bias,
        share_output,
        share_expand,
        share_expand_bias,
        share_shrink,
        share_vectors,
        new_input,
        new_bias,
        new_output,
        new_expand,
        new_expand_bias,
        new_shrink,
        new_vectors,
        mom_input,
        mom_bias,
        mom_output,
        mom_expand,
        mom_expand_bias,
        mom_shrink,
        mom_vectors,
    )


def solution(mesh):
    def body(*args):
        return on_device(mesh.shape[SHARD], mesh.shape[TENSOR], *args)

    return jax.shard_map(
        body,
        mesh=mesh,
        in_specs=(
            P(SHARD, None),
            P(SHARD, None),
            P(None, SHARD, TENSOR),
            P(None, None, SHARD, TENSOR),
            P(None, (TENSOR, SHARD)),
            P(None, None, (TENSOR, SHARD)),
            P(TENSOR, SHARD),
            P(None, TENSOR, SHARD),
            P(SHARD, TENSOR),
            P(None, SHARD, TENSOR),
            P((TENSOR, SHARD)),
            P(None, (TENSOR, SHARD)),
            P(TENSOR, SHARD),
            P(None, TENSOR, SHARD),
            P(None, SHARD),
            P(None, None, SHARD),
        ),
        out_specs=(
            P(SHARD, None),
            P(SHARD, None),
            P(None, SHARD, TENSOR),
            P(None, (TENSOR, SHARD)),
            P(TENSOR, SHARD),
            P(SHARD, TENSOR),
            P((TENSOR, SHARD)),
            P(TENSOR, SHARD),
            P(None, SHARD),
            P(None, SHARD, TENSOR),
            P(None, (TENSOR, SHARD)),
            P(TENSOR, SHARD),
            P(SHARD, TENSOR),
            P((TENSOR, SHARD)),
            P(TENSOR, SHARD),
            P(None, SHARD),
            P(None, None, SHARD, TENSOR),
            P(None, None, (TENSOR, SHARD)),
            P(None, TENSOR, SHARD),
            P(None, SHARD, TENSOR),
            P(None, (TENSOR, SHARD)),
            P(None, TENSOR, SHARD),
            P(None, None, SHARD),
        ),
        check_vma=False,
    )
```
